128 devices in a mesh: dp: 32 (over x, z, y_hi), crop: 4 (over y_lo, core).
Axes of the slice: x: 4, y: 4 (y_hi: 2, y_lo: 2; y = y_hi * 2 + y_lo), z: 4, core: 2. Of those that a mesh axis runs over, the one named last changes fastest.
Arguments:
- query_crops: bfloat16 [65536, 2048], P(('dp', 'crop')), may hold values from -6 to 6
- key_crops: bfloat16 [65536, 2048], P(('dp', 'crop')), may hold values from -43 to 43
- shuffle: int32 [65536], P(('dp', 'crop')), may hold values from 0 to 65535, as said below
- distractor_bank: bfloat16 [16384, 128], replicated, may hold values from -2.5 to 2.5
- query_inner: bfloat16 [2048, 2048], replicated, may hold values from -0.125 to 0.125
- query_outer: bfloat16 [2048, 128], replicated, may hold values from -0.125 to 0.125
- key_inner: bfloat16 [2048, 2048], replicated, may hold values from -0.125 to 0.125
- key_outer: bfloat16 [2048, 128], replicated, may hold values from -0.125 to 0.125
Outputs:
- grad_inner: float32 [2048, 2048], P(('dp', 'crop'))
- grad_outer: float32 [2048, 128], P(('dp', 'crop'))
The draws below stay inside these ranges and needn't reach their ends.
Inputs may be any that keep to these rules, and one draw needn't show every extreme that they name: `shuffle`: a permutation of the 65536 key crops; shuffled position t * 512 + s * 4 + j, for j below 4, takes a crop from rows s * 512 up to (s + 1) * 512 - 1.
All inputs are finite; a program needn't handle non-finite values.
Results may differ from the reference program's by a relative error of at most 0.008.
Values may be sent and summed in bfloat16 or wider, within the bound.
A program may use at most 192 MiB of HBM per device.

```python
import math
import jax
import jax.numpy as jnp
from jax import lax

D = 2048
HID = 2048
EMB = 128
QUEUE = 16384
ROWS = 512
TOTAL = 65536
N_DP = 32
N_CROP = 4


def draw_key_crops(key, part):
    group_count = TOTAL // ROWS
    seed_noise = jax.random.fold_in(key, 11)
    seed_scale = jax.random.fold_in(key, 12)
    seed_offset = jax.random.fold_in(key, 13)
    base_noise = jax.random.truncated_normal(seed_noise, -4.0, 4.0, (TOTAL, D), jnp.float32)
    row_scales = jnp.exp(jax.random.uniform(seed_scale, (TOTAL, 1), jnp.float32, 0.0, math.log(10.0)))
    offsets = jax.random.uniform(seed_offset, (group_count, 1, D), jnp.float32, -2.5, 2.5)
    values = (base_noise * row_scales).reshape(group_count, ROWS, D) + offsets
    return values.reshape(TOTAL, D).astype(jnp.bfloat16)


def draw_shuffle(key, part):
    group_count = TOTAL // ROWS
    per_peer = ROWS // group_count
    sources = jnp.arange(group_count, dtype=jnp.int32)

    def one_order(source):
        return jax.random.permutation(jax.random.fold_in(key, source), ROWS).astype(jnp.int32)
    orders = jax.vmap(one_order)(sources)
    blocks = orders.reshape(group_count, group_count, per_peer) + (sources * ROWS)[:, None, None]
    return jnp.transpose(blocks, (1, 0, 2)).reshape(TOTAL).astype(jnp.int32)


def block_levels(key, shape, cuts, low, high):
    def one(position, parts):
        draws = jax.random.uniform(jax.random.fold_in(jax.random.fold_in(key, 6), position), (parts,), jnp.float32, low / len(cuts), high / len(cuts))
        return jnp.repeat(jnp.exp(draws), shape[position] // parts).reshape((-1,) + (1,) * (len(shape) - position - 1))

    factor_of = one(*cuts[0])
    for cut in cuts[1:]:
        factor_of = factor_of * one(*cut)
    return factor_of


def normal_values(stream_key, shape, scale, reach, shards=(), held_as=jnp.bfloat16):
    entries = jax.random.normal(stream_key, shape, jnp.float32) * scale
    if len(shards) > 0:
        entries = block_levels(stream_key, shape, shards, -0.22, 0.18) * entries
    return jnp.clip(entries, min=-reach, max=reach).astype(held_as)


def setup_inputs(seed: int = 0) -> dict:
    streams_of = jax.random.split(jax.random.key(seed), 9)
    query_crops = normal_values(streams_of[0], (TOTAL, D), 1.0, 6.0, ((0, 128),))
    key_crops = draw_key_crops(jax.random.fold_in(streams_of[8], 71), 0)
    shuffle = draw_shuffle(jax.random.fold_in(streams_of[8], 71), 0)
    distractor_bank = normal_values(streams_of[3], (QUEUE, EMB), 0.3, 2.5)
    query_inner = normal_values(streams_of[4], (D, HID), D ** -0.5, 0.125)
    query_outer = normal_values(streams_of[5], (HID, EMB), HID ** -0.5, 0.125)
    key_inner = normal_values(streams_of[6], (D, HID), D ** -0.5, 0.125)
    key_outer = normal_values(streams_of[7], (HID, EMB), HID ** -0.5, 0.125)
    return {"query_crops": query_crops, "key_crops": key_crops, "shuffle": shuffle, "distractor_bank": distractor_bank, "query_inner": query_inner, "query_outer": query_outer, "key_inner": key_inner, "key_outer": key_outer}


sharpness_divisor = 0.2
loss_scale = 4096.0
bn_eps = 1e-05
norm_eps = 1e-06

def batch_stats(hidden):
    average = lax.optimization_barrier(jnp.mean(hidden, axis=0))
    variance = lax.optimization_barrier(jnp.mean(hidden * hidden, axis=0)) - average * average
    return (average, lax.rsqrt(variance + bn_eps))

def head_tail(normed, w_out):
    active = jnp.maximum(normed, 0.0).astype(jnp.bfloat16)
    projected = jnp.dot(active, w_out, preferred_element_type=jnp.float32)
    return projected * lax.rsqrt(lax.optimization_barrier(jnp.sum(projected * projected, axis=-1, keepdims=True)) + norm_eps)

def key_embed(crop_rows, w_in, w_out):
    hidden = jnp.dot(crop_rows, w_in, preferred_element_type=jnp.float32)
    average, inv_std = batch_stats(hidden)
    return head_tail((hidden - average) * inv_std, w_out)

def query_grads(crop_rows, matching_targets, distractor_bank, w_in, w_out, all_rows):
    hidden = jnp.dot(crop_rows, w_in, preferred_element_type=jnp.float32)
    average, inv_std = batch_stats(hidden)
    normed = (hidden - average) * inv_std
    active = jnp.maximum(normed, 0.0).astype(jnp.bfloat16)
    projected = jnp.dot(active, w_out, preferred_element_type=jnp.float32)
    inv_len = lax.rsqrt(lax.optimization_barrier(jnp.sum(projected * projected, axis=-1, keepdims=True)) + norm_eps)
    probe_features = projected * inv_len
    matching_similarity = lax.optimization_barrier(jnp.sum(probe_features * matching_targets, axis=-1, keepdims=True)) / sharpness_divisor
    distractor_similarities = lax.dot_general(probe_features.astype(jnp.bfloat16), distractor_bank, (((1,), (1,)), ((), ())), preferred_element_type=jnp.float32) / sharpness_divisor
    exp_pos = jnp.exp(matching_similarity)
    exp_neg = jnp.exp(distractor_similarities)
    total_exp = exp_pos + lax.optimization_barrier(jnp.sum(exp_neg, axis=-1, keepdims=True))
    scale_coef = loss_scale / all_rows
    matching_similarity_slope = scale_coef * (exp_pos / total_exp - 1.0)
    distractor_similarity_slope = (scale_coef * exp_neg / total_exp).astype(jnp.bfloat16)
    probe_feature_slope = (matching_similarity_slope * matching_targets + jnp.dot(distractor_similarity_slope, distractor_bank, preferred_element_type=jnp.float32)) / sharpness_divisor
    d_proj = ((probe_feature_slope - probe_features * lax.optimization_barrier(jnp.sum(probe_feature_slope * probe_features, axis=-1, keepdims=True))) * inv_len).astype(jnp.bfloat16)
    grad_out = lax.dot_general(active, d_proj, (((0,), (0,)), ((), ())), preferred_element_type=jnp.float32)
    d_act = lax.dot_general(d_proj, w_out, (((1,), (1,)), ((), ())), preferred_element_type=jnp.float32)
    d_norm = jnp.where(normed > 0.0, d_act, 0.0)
    d_hidden = inv_std * (d_norm - lax.optimization_barrier(jnp.mean(d_norm, axis=0)) - normed * lax.optimization_barrier(jnp.mean(d_norm * normed, axis=0)))
    grad_in = lax.dot_general(crop_rows, d_hidden.astype(jnp.bfloat16), (((0,), (0,)), ((), ())), preferred_element_type=jnp.float32)
    return (grad_in, grad_out)

def reference(query_crops, key_crops, shuffle, distractor_bank, query_inner, query_outer, key_inner, key_outer):
    group_count = N_DP * N_CROP
    shuffled = key_crops[shuffle].reshape(group_count, ROWS, D)

    def embed_group(group_rows):
        return key_embed(group_rows, key_inner, key_outer)
    embedded = lax.map(embed_group, shuffled).reshape(TOTAL, EMB)
    matching_targets = jnp.zeros((TOTAL, EMB), jnp.float32).at[shuffle].set(embedded)
    all_rows = float(TOTAL)

    def accumulate(running, block_pair):
        grad_in, grad_out = query_grads(block_pair[0], block_pair[1], distractor_bank, query_inner, query_outer, all_rows)
        return ((running[0] + grad_in, running[1] + grad_out), None)
    initial = (jnp.zeros((D, HID), jnp.float32), jnp.zeros((HID, EMB), jnp.float32))
    (grad_inner, grad_outer), _ = lax.scan(accumulate, initial, (query_crops.reshape(group_count, ROWS, D), matching_targets.reshape(group_count, ROWS, EMB)))
    return (grad_inner, grad_outer)
```

```python
import jax
import jax.numpy as jnp
from jax import lax
from jax.sharding import PartitionSpec as P

sharpness_divisor = 0.2
loss_scale = 4096.0
bn_eps = 1e-05
norm_eps = 1e-06


def batch_stats(hidden):
    average = jnp.mean(hidden, axis=0)
    variance = jnp.mean(hidden * hidden, axis=0) - average * average
    return (average, lax.rsqrt(variance + bn_eps))


def head_tail(normed, w_out):
    active = jnp.maximum(normed, 0.0).astype(jnp.bfloat16)
    projected = jnp.dot(active, w_out, preferred_element_type=jnp.float32)
    return projected * lax.rsqrt(jnp.sum(projected * projected, axis=-1, keepdims=True) + norm_eps)


def key_embed(crop_rows, w_in, w_out):
    hidden = jnp.dot(crop_rows, w_in, preferred_element_type=jnp.float32)
    average, inv_std = batch_stats(hidden)
    return head_tail((hidden - average) * inv_std, w_out)


def query_grads(crop_rows, matching_targets, distractor_bank, w_in, w_out, all_rows):
    hidden = jnp.dot(crop_rows, w_in, preferred_element_type=jnp.float32)
    average, inv_std = batch_stats(hidden)
    normed = (hidden - average) * inv_std
    active = jnp.maximum(normed, 0.0).astype(jnp.bfloat16)
    projected = jnp.dot(active, w_out, preferred_element_type=jnp.float32)
    inv_len = lax.rsqrt(jnp.sum(projected * projected, axis=-1, keepdims=True) + norm_eps)
    probe_features = projected * inv_len
    matching_similarity = (
        jnp.sum(probe_features * matching_targets, axis=-1, keepdims=True) / sharpness_divisor
    )
    distractor_similarities = (
        lax.dot_general(
            probe_features.astype(jnp.bfloat16),
            distractor_bank,
            (((1,), (1,)), ((), ())),
            preferred_element_type=jnp.float32,
        )
        / sharpness_divisor
    )
    exp_pos = jnp.exp(matching_similarity)
    exp_neg = jnp.exp(distractor_similarities)
    total_exp = exp_pos + jnp.sum(exp_neg, axis=-1, keepdims=True)
    scale_coef = loss_scale / all_rows
    matching_similarity_slope = scale_coef * (exp_pos / total_exp - 1.0)
    distractor_similarity_slope = (scale_coef * exp_neg / total_exp).astype(jnp.bfloat16)
    probe_feature_slope = (
        matching_similarity_slope * matching_targets
        + jnp.dot(distractor_similarity_slope, distractor_bank, preferred_element_type=jnp.float32)
    ) / sharpness_divisor
    d_proj = (
        (
            probe_feature_slope
            - probe_features * jnp.sum(probe_feature_slope * probe_features, axis=-1, keepdims=True)
        )
        * inv_len
    ).astype(jnp.bfloat16)
    grad_out = lax.dot_general(
        active, d_proj, (((0,), (0,)), ((), ())), preferred_element_type=jnp.float32
    )
    d_act = lax.dot_general(
        d_proj, w_out, (((1,), (1,)), ((), ())), preferred_element_type=jnp.float32
    )
    d_norm = jnp.where(normed > 0.0, d_act, 0.0)
    d_hidden = inv_std * (
        d_norm - jnp.mean(d_norm, axis=0) - normed * jnp.mean(d_norm * normed, axis=0)
    )
    grad_in = lax.dot_general(
        crop_rows,
        d_hidden.astype(jnp.bfloat16),
        (((0,), (0,)), ((), ())),
        preferred_element_type=jnp.float32,
    )
    return (grad_in, grad_out)


def per_device(
    query_crops, key_crops, shuffle, distractor_bank, query_inner, query_outer, key_inner, key_outer
):
    group_count = lax.axis_size(("dp", "crop"))
    row_count = query_crops.shape[0]
    per_peer = row_count // group_count
    all_rows = float(row_count * group_count)
    wanted = (shuffle % row_count).reshape(group_count, per_peer)
    requested = lax.all_to_all(wanted, ("dp", "crop"), split_axis=0, concat_axis=0, tiled=True)
    flat_req = requested.reshape(-1)
    outgoing = key_crops[flat_req].reshape(group_count, per_peer, key_crops.shape[1])
    incoming = lax.all_to_all(
        outgoing, ("dp", "crop"), split_axis=0, concat_axis=0, tiled=True
    ).reshape(row_count, key_crops.shape[1])
    embedded = key_embed(incoming, key_inner, key_outer).reshape(
        group_count, per_peer, key_outer.shape[1]
    )
    returned = lax.all_to_all(
        embedded, ("dp", "crop"), split_axis=0, concat_axis=0, tiled=True
    ).reshape(row_count, key_outer.shape[1])
    matching_targets = (
        jnp.zeros((row_count, returned.shape[1]), jnp.float32).at[flat_req].set(returned)
    )
    grad_in, grad_out = query_grads(
        query_crops, matching_targets, distractor_bank, query_inner, query_outer, all_rows
    )
    width_in, width_out = grad_in.shape[1], grad_out.shape[1]
    slices = (
        jnp.concatenate([grad_in, grad_out], axis=1)
        .astype(jnp.bfloat16)
        .reshape(group_count, grad_in.shape[0] // group_count, width_in + width_out)
    )
    partials = lax.all_to_all(slices, ("dp", "crop"), split_axis=0, concat_axis=0, tiled=True)
    summed = jnp.sum(partials.astype(jnp.float32), axis=0)
    grad_in, grad_out = summed[:, :width_in], summed[:, width_in:]
    return (grad_in, grad_out)


def solution(mesh):
    placed = (
        P(("dp", "crop"), None),
        P(("dp", "crop"), None),
        P(("dp", "crop")),
        P(),
        P(),
        P(),
        P(),
        P(),
    )
    return jax.shard_map(
        per_device,
        mesh=mesh,
        in_specs=placed,
        out_specs=(P(("dp", "crop"), None), P(("dp", "crop"), None)),
        check_vma=False,
    )
```

```python
import functools
import jax
import jax.numpy as jnp
from jax import lax
from jax.experimental import pallas as pl
from jax.experimental.pallas import tpu as pltpu
from jax.sharding import PartitionSpec as P

sharpness_divisor = 0.2
loss_scale = 4096.0
bn_eps = 1e-05
norm_eps = 1e-06


MESH = pl.DeviceIdType.MESH
CHUNK = 16
LANES = 128
TURNS = (("x", 1), ("y", 1), ("z", 1), ("x", 3), ("y", 3), ("z", 3))
AXES = ("x", "y", "z")


def place():
    dp, crop = lax.axis_index("dp"), lax.axis_index("crop")
    return {
        "x": dp // 8,
        "z": (dp // 2) % 4,
        "y": (dp % 2) * 2 + crop // 2,
        "core": crop % 2,
    }


def device_of(at):
    return (at["x"] * 8 + at["z"] * 2 + at["y"] // 2, (at["y"] % 2) * 2 + at["core"])


def mirrored(v, u):
    return (v, v + 1 - 2 * (v % 2), (v + 2) % 4, 3 - v)[u]


def partner(at, turn):
    if turn is None:
        return device_of({**at, "core": 1 - at["core"]})
    axis, flip = turn
    return device_of({**at, axis: mirrored(at[axis], flip)})


def greet(at):
    barrier = pltpu.get_barrier_semaphore()
    for turn in (None,) + TURNS:
        pl.semaphore_signal(barrier, inc=1, device_id=partner(at, turn), device_id_type=MESH)
    pl.semaphore_wait(barrier, 1 + len(TURNS))


def plan_of(kind):
    held = {a: [0, 1, 2, 3] for a in AXES}
    hops = []
    for k in range(6):
        axis, flip = TURNS[(kind + k) % 6]
        now = held[axis]
        if len(now) == 4:
            sent = [1, 2] if flip == 1 else [3, 2]
        else:
            sent = [flip]
        kept = [u ^ flip for u in sent]
        dims = tuple(len(held[a]) for a in AXES)
        hops.append(
            (dims, AXES.index(axis), [now.index(u) for u in kept], [now.index(u) for u in sent])
        )
        held[axis] = kept
    return hops


PLANS = [plan_of(kind) for kind in range(6)]


def grads_kernel(tiles, xt_ref, dh_ref, go_ref, gi_out, go_out, xp, *rest):
    acc, send, recv = rest[0:7], rest[7:14], rest[14:21]
    send_sem, recv_sem = rest[21], rest[22]
    slots = tiles + 2
    at = place()
    greet(at)

    def copy(k, t, kind):
        turn = None if k == 0 else TURNS[(kind + k - 1) % 6]
        return pltpu.make_async_remote_copy(
            src_ref=send[k].at[t],
            dst_ref=recv[k].at[t],
            send_sem=send_sem.at[k, t],
            recv_sem=recv_sem.at[k, t],
            device_id=partner(at, turn),
            device_id_type=MESH,
        )

    def combine(k, t, kind):
        copy(k, t, kind).wait_recv()
        total = acc[k][t] + recv[k][t].astype(jnp.float32)
        if k == 6:
            return total[0]
        dims, axis, kept, sent = PLANS[kind][k]
        total = total.reshape(dims + (CHUNK, LANES))
        out_dims = tuple(n // 2 if i == axis else n for i, n in enumerate(dims))

        def pick(positions):
            parts = [lax.slice_in_dim(total, p, p + 1, axis=axis) for p in positions]
            joined = parts[0] if len(parts) == 1 else jnp.concatenate(parts, axis=axis)
            return joined.reshape((-1, CHUNK, LANES))

        send[k + 1][t] = pick(sent).astype(jnp.bfloat16)
        acc[k + 1][t] = pick(kept)
        copy(k + 1, t, kind).start()

    rows = {}
    index = 0
    for far in (1, 0):
        core = at["core"] if far == 0 else 1 - at["core"]
        for ux in range(4):
            for uy in range(4):
                for uz in range(4):
                    wx, wy, wz = (mirrored(at[a], u) for a, u in zip(AXES, (ux, uy, uz)))
                    row = pl.multiple_of((((wx * 4 + wz) * 4 + wy) * 2 + core) * CHUNK, CHUNK)
                    rows[index] = row
                    xp[index * CHUNK : (index + 1) * CHUNK, :] = xt_ref[pl.ds(row, CHUNK), :]
                    index += 1

    def outer():
        for i in range(64):
            send[0][tiles, i] = go_ref[pl.ds(rows[i], CHUNK), :].astype(jnp.bfloat16)
            acc[0][tiles, i] = go_ref[pl.ds(rows[64 + i], CHUNK), :]
        send[0][tiles + 1] = jnp.zeros((64, CHUNK, LANES), jnp.bfloat16)
        acc[0][tiles + 1] = jnp.zeros((64, CHUNK, LANES), jnp.float32)
        for t in (tiles, tiles + 1):
            copy(0, t, t % 6).start()

    def inner(g):
        right = dh_ref[:, 2 * g * LANES : (2 * g + 2) * LANES]

        def block(far, b):
            left = xp[pl.ds(pl.multiple_of((far * 4 + b) * 256, 256), 256), :]
            part = jnp.dot(left, right, preferred_element_type=jnp.float32)
            for h in range(2):
                half = part[:, h * LANES : (h + 1) * LANES].reshape(16, CHUNK, LANES)
                where = pl.ds(b * 16, 16)
                if far == 0:
                    send[0][2 * g + h, where] = half.astype(jnp.bfloat16)
                else:
                    acc[0][2 * g + h, where] = half

        @pl.loop(0, 4)
        def _(b):
            block(0, b)

        for h in range(2):
            copy(0, 2 * g + h, (2 * g + h) % 6).start()

        @pl.loop(0, 4)
        def _(b):
            block(1, b)

    pairs = slots // 2
    for g in range(pairs + 1):
        if g < pairs - 1:
            inner(g)
        elif g == pairs - 1:
            outer()
        if g >= 1:
            for h in range(2):
                t = 2 * (g - 1) + h
                combine(0, t, t % 6)

    for k in range(1, 6):

        @pl.loop(0, slots // 6)
        def _(r, k=k):
            for kind in range(6):
                combine(k, r * 6 + kind, kind)

    for t in range(slots - 1):
        if t < tiles:
            gi_out[:, t * LANES : (t + 1) * LANES] = combine(6, t, t % 6)
        else:
            go_out[...] = combine(6, t, t % 6)
    combine(6, slots - 1, (slots - 1) % 6)

    for k in range(7):

        @pl.loop(0, slots // 6)
        def _(r, k=k):
            for kind in range(6):
                copy(k, r * 6 + kind, kind).wait_send()


def summed_grads(crops_t, d_hidden, grad_outer):
    depth, batch = crops_t.shape
    width = d_hidden.shape[1]
    tiles = width // LANES
    slots = tiles + 2

    def slabs(dtype):
        return [pltpu.VMEM((slots, 64 >> k, CHUNK, LANES), dtype) for k in range(7)]

    return pl.pallas_call(
        functools.partial(grads_kernel, tiles),
        out_shape=(
            jax.ShapeDtypeStruct((CHUNK, width), jnp.float32),
            jax.ShapeDtypeStruct((CHUNK, LANES), jnp.float32),
        ),
        in_specs=[pl.BlockSpec(memory_space=pltpu.VMEM)] * 3,
        out_specs=[pl.BlockSpec(memory_space=pltpu.VMEM)] * 2,
        scratch_shapes=[pltpu.VMEM((depth, batch), jnp.bfloat16)]
        + slabs(jnp.float32)
        + [pltpu.VMEM((slots, 64, CHUNK, LANES), jnp.bfloat16)]
        + slabs(jnp.bfloat16)[1:]
        + slabs(jnp.bfloat16)
        + [pltpu.SemaphoreType.DMA((7, slots)), pltpu.SemaphoreType.DMA((7, slots))],
        compiler_params=pltpu.CompilerParams(
            collective_id=0, has_side_effects=True, vmem_limit_bytes=60 << 20
        ),
    )(crops_t, d_hidden, grad_outer)


def batch_stats(hidden):
    average = jnp.mean(hidden, axis=0)
    variance = jnp.mean(hidden * hidden, axis=0) - average * average
    return (average, lax.rsqrt(variance + bn_eps))


def head_tail(normed, w_out):
    active = jnp.maximum(normed, 0.0).astype(jnp.bfloat16)
    projected = jnp.dot(active, w_out, preferred_element_type=jnp.float32)
    return projected * lax.rsqrt(jnp.sum(projected * projected, axis=-1, keepdims=True) + norm_eps)


def key_embed(crop_rows, w_in, w_out):
    hidden = jnp.dot(crop_rows, w_in, preferred_element_type=jnp.float32)
    average, inv_std = batch_stats(hidden)
    return head_tail((hidden - average) * inv_std, w_out)


def query_grads(crop_rows, matching_targets, distractor_bank, w_in, w_out, all_rows):
    hidden = jnp.dot(crop_rows, w_in, preferred_element_type=jnp.float32)
    average, inv_std = batch_stats(hidden)
    normed = (hidden - average) * inv_std
    active = jnp.maximum(normed, 0.0).astype(jnp.bfloat16)
    projected = jnp.dot(active, w_out, preferred_element_type=jnp.float32)
    inv_len = lax.rsqrt(jnp.sum(projected * projected, axis=-1, keepdims=True) + norm_eps)
    probe_features = projected * inv_len
    matching_similarity = (
        jnp.sum(probe_features * matching_targets, axis=-1, keepdims=True) / sharpness_divisor
    )
    distractor_similarities = (
        lax.dot_general(
            probe_features.astype(jnp.bfloat16),
            distractor_bank,
            (((1,), (1,)), ((), ())),
            preferred_element_type=jnp.float32,
        )
        / sharpness_divisor
    )
    exp_pos = jnp.exp(matching_similarity)
    exp_neg = jnp.exp(distractor_similarities)
    total_exp = exp_pos + jnp.sum(exp_neg, axis=-1, keepdims=True)
    scale_coef = loss_scale / all_rows
    matching_similarity_slope = scale_coef * (exp_pos / total_exp - 1.0)
    distractor_similarity_slope = (scale_coef * exp_neg / total_exp).astype(jnp.bfloat16)
    probe_feature_slope = (
        matching_similarity_slope * matching_targets
        + jnp.dot(distractor_similarity_slope, distractor_bank, preferred_element_type=jnp.float32)
    ) / sharpness_divisor
    d_proj = (
        (
            probe_feature_slope
            - probe_features * jnp.sum(probe_feature_slope * probe_features, axis=-1, keepdims=True)
        )
        * inv_len
    ).astype(jnp.bfloat16)
    grad_out = lax.dot_general(
        active, d_proj, (((0,), (0,)), ((), ())), preferred_element_type=jnp.float32
    )
    d_act = lax.dot_general(
        d_proj, w_out, (((1,), (1,)), ((), ())), preferred_element_type=jnp.float32
    )
    d_norm = jnp.where(normed > 0.0, d_act, 0.0)
    d_hidden = inv_std * (
        d_norm - jnp.mean(d_norm, axis=0) - normed * jnp.mean(d_norm * normed, axis=0)
    )
    return summed_grads(crop_rows.T, d_hidden.astype(jnp.bfloat16), grad_out)


def per_device(
    query_crops, key_crops, shuffle, distractor_bank, query_inner, query_outer, key_inner, key_outer
):
    group_count = lax.axis_size(("dp", "crop"))
    row_count = query_crops.shape[0]
    per_peer = row_count // group_count
    all_rows = float(row_count * group_count)
    wanted = (shuffle % row_count).reshape(group_count, per_peer)
    requested = lax.all_to_all(wanted, ("dp", "crop"), split_axis=0, concat_axis=0, tiled=True)
    flat_req = requested.reshape(-1)
    outgoing = key_crops[flat_req].reshape(group_count, per_peer, key_crops.shape[1])
    incoming = lax.all_to_all(
        outgoing, ("dp", "crop"), split_axis=0, concat_axis=0, tiled=True
    ).reshape(row_count, key_crops.shape[1])
    embedded = key_embed(incoming, key_inner, key_outer).reshape(
        group_count, per_peer, key_outer.shape[1]
    )
    returned = lax.all_to_all(
        embedded, ("dp", "crop"), split_axis=0, concat_axis=0, tiled=True
    ).reshape(row_count, key_outer.shape[1])
    matching_targets = (
        jnp.zeros((row_count, returned.shape[1]), jnp.float32).at[flat_req].set(returned)
    )
    grad_in, grad_out = query_grads(
        query_crops, matching_targets, distractor_bank, query_inner, query_outer, all_rows
    )
    return (grad_in, grad_out)


def solution(mesh):
    placed = (
        P(("dp", "crop"), None),
        P(("dp", "crop"), None),
        P(("dp", "crop")),
        P(),
        P(),
        P(),
        P(),
        P(),
    )
    return jax.shard_map(
        per_device,
        mesh=mesh,
        in_specs=placed,
        out_specs=(P(("dp", "crop"), None), P(("dp", "crop"), None)),
        check_vma=False,
    )
```

```python
import functools
import math
import jax
import jax.numpy as jnp
from jax import lax
from jax.experimental import pallas as pl
from jax.experimental.pallas import tpu as pltpu
from jax.sharding import PartitionSpec as P

sharpness_divisor = 0.2
loss_scale = 4096.0
bn_eps = 1e-05
norm_eps = 1e-06
EXP2_SCALE = math.log2(math.e) / sharpness_divisor


MESH = pl.DeviceIdType.MESH
CHUNK = 16
LANES = 128
TURNS = (("x", 1), ("y", 1), ("z", 1), ("x", 3), ("y", 3), ("z", 3))
AXES = ("x", "y", "z")


def place():
    dp, crop = lax.axis_index("dp"), lax.axis_index("crop")
    return {
        "x": dp // 8,
        "z": (dp // 2) % 4,
        "y": (dp % 2) * 2 + crop // 2,
        "core": crop % 2,
    }


def device_of(at):
    return (at["x"] * 8 + at["z"] * 2 + at["y"] // 2, (at["y"] % 2) * 2 + at["core"])


def mirrored(v, u):
    return (v, v + 1 - 2 * (v % 2), (v + 2) % 4, 3 - v)[u]


def partner(at, turn):
    if turn is None:
        return device_of({**at, "core": 1 - at["core"]})
    axis, flip = turn
    return device_of({**at, axis: mirrored(at[axis], flip)})


def greet(at):
    barrier = pltpu.get_barrier_semaphore()
    for turn in (None,) + TURNS:
        pl.semaphore_signal(barrier, inc=1, device_id=partner(at, turn), device_id_type=MESH)
    pl.semaphore_wait(barrier, 1 + len(TURNS))


def plan_of(kind):
    held = {a: [0, 1, 2, 3] for a in AXES}
    hops = []
    for k in range(6):
        axis, flip = TURNS[(kind + k) % 6]
        now = held[axis]
        if len(now) == 4:
            sent = [1, 2] if flip == 1 else [3, 2]
        else:
            sent = [flip]
        kept = [u ^ flip for u in sent]
        dims = tuple(len(held[a]) for a in AXES)
        hops.append(
            (dims, AXES.index(axis), [now.index(u) for u in kept], [now.index(u) for u in sent])
        )
        held[axis] = kept
    return hops


PLANS = [plan_of(kind) for kind in range(6)]


def grads_kernel(tiles, xt_ref, dh_ref, go_ref, gi_out, go_out, xp, *rest):
    acc, send, recv = rest[0:7], rest[7:14], rest[14:21]
    send_sem, recv_sem = rest[21], rest[22]
    slots = tiles + 2
    at = place()
    greet(at)

    def copy(k, t, kind):
        turn = None if k == 0 else TURNS[(kind + k - 1) % 6]
        return pltpu.make_async_remote_copy(
            src_ref=send[k].at[t],
            dst_ref=recv[k].at[t],
            send_sem=send_sem.at[k, t],
            recv_sem=recv_sem.at[k, t],
            device_id=partner(at, turn),
            device_id_type=MESH,
        )

    def combine(k, t, kind):
        copy(k, t, kind).wait_recv()
        total = acc[k][t] + recv[k][t].astype(jnp.float32)
        if k == 6:
            return total[0]
        dims, axis, kept, sent = PLANS[kind][k]
        total = total.reshape(dims + (CHUNK, LANES))
        out_dims = tuple(n // 2 if i == axis else n for i, n in enumerate(dims))

        def pick(positions):
            parts = [lax.slice_in_dim(total, p, p + 1, axis=axis) for p in positions]
            joined = parts[0] if len(parts) == 1 else jnp.concatenate(parts, axis=axis)
            return joined.reshape((-1, CHUNK, LANES))

        send[k + 1][t] = pick(sent).astype(jnp.bfloat16)
        acc[k + 1][t] = pick(kept)
        copy(k + 1, t, kind).start()

    rows = {}
    index = 0
    for far in (1, 0):
        core = at["core"] if far == 0 else 1 - at["core"]
        for ux in range(4):
            for uy in range(4):
                for uz in range(4):
                    wx, wy, wz = (mirrored(at[a], u) for a, u in zip(AXES, (ux, uy, uz)))
                    row = pl.multiple_of((((wx * 4 + wz) * 4 + wy) * 2 + core) * CHUNK, CHUNK)
                    rows[index] = row
                    xp[index * CHUNK : (index + 1) * CHUNK, :] = xt_ref[pl.ds(row, CHUNK), :]
                    index += 1

    def outer():
        for i in range(64):
            send[0][tiles, i] = go_ref[pl.ds(rows[i], CHUNK), :].astype(jnp.bfloat16)
            acc[0][tiles, i] = go_ref[pl.ds(rows[64 + i], CHUNK), :]
        send[0][tiles + 1] = jnp.zeros((64, CHUNK, LANES), jnp.bfloat16)
        acc[0][tiles + 1] = jnp.zeros((64, CHUNK, LANES), jnp.float32)
        for t in (tiles, tiles + 1):
            copy(0, t, t % 6).start()

    def inner(g):
        right = dh_ref[:, 2 * g * LANES : (2 * g + 2) * LANES]

        def block(far, b):
            left = xp[pl.ds(pl.multiple_of((far * 4 + b) * 256, 256), 256), :]
            part = jnp.dot(left, right, preferred_element_type=jnp.float32)
            for h in range(2):
                half = part[:, h * LANES : (h + 1) * LANES].reshape(16, CHUNK, LANES)
                where = pl.ds(b * 16, 16)
                if far == 0:
                    send[0][2 * g + h, where] = half.astype(jnp.bfloat16)
                else:
                    acc[0][2 * g + h, where] = half

        @pl.loop(0, 4)
        def _(b):
            block(0, b)

        for h in range(2):
            copy(0, 2 * g + h, (2 * g + h) % 6).start()

        @pl.loop(0, 4)
        def _(b):
            block(1, b)

    pairs = slots // 2
    for g in range(pairs + 1):
        if g < pairs - 1:
            inner(g)
        elif g == pairs - 1:
            outer()
        if g >= 1:
            for h in range(2):
                t = 2 * (g - 1) + h
                combine(0, t, t % 6)

    for k in range(1, 6):

        @pl.loop(0, slots // 6)
        def _(r, k=k):
            for kind in range(6):
                combine(k, r * 6 + kind, kind)

    for t in range(slots - 1):
        if t < tiles:
            gi_out[:, t * LANES : (t + 1) * LANES] = combine(6, t, t % 6)
        else:
            go_out[...] = combine(6, t, t % 6)
    combine(6, slots - 1, (slots - 1) % 6)

    for k in range(7):

        @pl.loop(0, slots // 6)
        def _(r, k=k):
            for kind in range(6):
                copy(k, r * 6 + kind, kind).wait_send()


def summed_grads(crops_t, d_hidden, grad_outer):
    depth, batch = crops_t.shape
    width = d_hidden.shape[1]
    tiles = width // LANES
    slots = tiles + 2

    def slabs(dtype):
        return [pltpu.VMEM((slots, 64 >> k, CHUNK, LANES), dtype) for k in range(7)]

    return pl.pallas_call(
        functools.partial(grads_kernel, tiles),
        out_shape=(
            jax.ShapeDtypeStruct((CHUNK, width), jnp.float32),
            jax.ShapeDtypeStruct((CHUNK, LANES), jnp.float32),
        ),
        in_specs=[pl.BlockSpec(memory_space=pltpu.VMEM)] * 3,
        out_specs=[pl.BlockSpec(memory_space=pltpu.VMEM)] * 2,
        scratch_shapes=[pltpu.VMEM((depth, batch), jnp.bfloat16)]
        + slabs(jnp.float32)
        + [pltpu.VMEM((slots, 64, CHUNK, LANES), jnp.bfloat16)]
        + slabs(jnp.bfloat16)[1:]
        + slabs(jnp.bfloat16)
        + [pltpu.SemaphoreType.DMA((7, slots)), pltpu.SemaphoreType.DMA((7, slots))],
        compiler_params=pltpu.CompilerParams(
            collective_id=0, has_side_effects=True, vmem_limit_bytes=60 << 20
        ),
    )(crops_t, d_hidden, grad_outer)


def negatives_kernel(chunk, q_ref, bank_ref, total_ref, pull_ref):
    @pl.when(pl.program_id(0) == 0)
    def _():
        total_ref[...] = jnp.zeros_like(total_ref)
        pull_ref[...] = jnp.zeros_like(pull_ref)

    keys = bank_ref[...]
    for start in range(0, q_ref.shape[0], chunk):
        rows = slice(start, start + chunk)
        sims = lax.dot_general(
            q_ref[rows, :].astype(jnp.bfloat16), keys, (((1,), (1,)), ((), ())), preferred_element_type=jnp.float32
        )
        quarter = jnp.exp2(sims * EXP2_SCALE - 2.0)
        partial = quarter[:, 0:LANES]
        for c in range(LANES, quarter.shape[1], LANES):
            partial = partial + quarter[:, c : c + LANES]
        total_ref[rows, :] += partial
        pull_ref[rows, :] += jnp.dot(
            quarter.astype(jnp.bfloat16), keys, preferred_element_type=jnp.float32
        )


def negatives(probe_features, distractor_bank, block=4096, chunk=256):
    rows, emb = probe_features.shape
    keys = distractor_bank.shape[0]
    whole = pl.BlockSpec((rows, emb), lambda i: (0, 0))
    return pl.pallas_call(
        functools.partial(negatives_kernel, chunk),
        grid=(keys // block,),
        out_shape=(jax.ShapeDtypeStruct((rows, emb), jnp.float32),) * 2,
        in_specs=[whole, pl.BlockSpec((block, emb), lambda i: (i, 0))],
        out_specs=[whole, whole],
        cost_estimate=pl.CostEstimate(
            flops=4 * rows * keys * emb, bytes_accessed=2 * keys * emb, transcendentals=rows * keys
        ),
        compiler_params=pltpu.CompilerParams(vmem_limit_bytes=60 << 20),
    )(probe_features, distractor_bank)


def batch_stats(hidden):
    average = jnp.mean(hidden, axis=0)
    variance = jnp.mean(hidden * hidden, axis=0) - average * average
    return (average, lax.rsqrt(variance + bn_eps))


def head_tail(normed, w_out):
    active = jnp.maximum(normed, 0.0).astype(jnp.bfloat16)
    projected = jnp.dot(active, w_out, preferred_element_type=jnp.float32)
    return projected * lax.rsqrt(jnp.sum(projected * projected, axis=-1, keepdims=True) + norm_eps)


def key_embed(crop_rows, w_in, w_out):
    hidden = jnp.dot(crop_rows, w_in, preferred_element_type=jnp.float32)
    average, inv_std = batch_stats(hidden)
    return head_tail((hidden - average) * inv_std, w_out)


def query_forward(crop_rows, w_in, w_out):
    hidden = jnp.dot(crop_rows, w_in, preferred_element_type=jnp.float32)
    average, inv_std = batch_stats(hidden)
    normed = (hidden - average) * inv_std
    active = jnp.maximum(normed, 0.0).astype(jnp.bfloat16)
    projected = jnp.dot(active, w_out, preferred_element_type=jnp.float32)
    inv_len = lax.rsqrt(jnp.sum(projected * projected, axis=-1, keepdims=True) + norm_eps)
    return (normed, active, inv_std, inv_len, projected * inv_len)


def query_grads(crops_t, forward, lane_totals, pull, matching_targets, w_out, all_rows):
    normed, active, inv_std, inv_len, probe_features = forward
    matching_similarity = (
        jnp.sum(probe_features * matching_targets, axis=-1, keepdims=True) / sharpness_divisor
    )
    exp_pos = jnp.exp(matching_similarity) * 0.25
    total_exp = exp_pos + jnp.sum(lane_totals, axis=-1, keepdims=True)
    scale_coef = loss_scale / all_rows
    matching_similarity_slope = scale_coef * (exp_pos / total_exp - 1.0)
    probe_feature_slope = (
        matching_similarity_slope * matching_targets + scale_coef * pull / total_exp
    ) / sharpness_divisor
    d_proj = (
        (
            probe_feature_slope
            - probe_features * jnp.sum(probe_feature_slope * probe_features, axis=-1, keepdims=True)
        )
        * inv_len
    ).astype(jnp.bfloat16)
    grad_out = lax.dot_general(
        active, d_proj, (((0,), (0,)), ((), ())), preferred_element_type=jnp.float32
    )
    d_act = lax.dot_general(
        d_proj, w_out, (((1,), (1,)), ((), ())), preferred_element_type=jnp.float32
    )
    d_norm = jnp.where(normed > 0.0, d_act, 0.0)
    d_hidden = inv_std * (
        d_norm - jnp.mean(d_norm, axis=0) - normed * jnp.mean(d_norm * normed, axis=0)
    )
    return summed_grads(crops_t, d_hidden.astype(jnp.bfloat16), grad_out)


def per_device(
    query_crops, key_crops, shuffle, distractor_bank, query_inner, query_outer, key_inner, key_outer
):
    group_count = lax.axis_size(("dp", "crop"))
    row_count = query_crops.shape[0]
    per_peer = row_count // group_count
    all_rows = float(row_count * group_count)
    wanted = (shuffle % row_count).reshape(group_count, per_peer)
    requested = lax.all_to_all(wanted, ("dp", "crop"), split_axis=0, concat_axis=0, tiled=True)
    flat_req = requested.reshape(-1)
    outgoing = key_crops[flat_req].reshape(group_count, per_peer, key_crops.shape[1])
    incoming = lax.all_to_all(outgoing, ("dp", "crop"), split_axis=0, concat_axis=0, tiled=True)
    forward = query_forward(query_crops, query_inner, query_outer)
    crops_t = query_crops.T
    lane_totals, pull = negatives(forward[4], distractor_bank)
    incoming, lane_totals, pull, crops_t = lax.optimization_barrier(
        (incoming, lane_totals, pull, crops_t)
    )
    embedded = key_embed(
        incoming.reshape(row_count, key_crops.shape[1]), key_inner, key_outer
    ).reshape(group_count, per_peer, key_outer.shape[1])
    returned = lax.all_to_all(
        embedded, ("dp", "crop"), split_axis=0, concat_axis=0, tiled=True
    ).reshape(row_count, key_outer.shape[1])
    matching_targets = (
        jnp.zeros((row_count, returned.shape[1]), jnp.float32).at[flat_req].set(returned)
    )
    return query_grads(
        crops_t, forward, lane_totals, pull, matching_targets, query_outer, all_rows
    )


def solution(mesh):
    placed = (
        P(("dp", "crop"), None),
        P(("dp", "crop"), None),
        P(("dp", "crop")),
        P(),
        P(),
        P(),
        P(),
        P(),
    )
    return jax.shard_map(
        per_device,
        mesh=mesh,
        in_specs=placed,
        out_specs=(P(("dp", "crop"), None), P(("dp", "crop"), None)),
        check_vma=False,
    )
```

```python
import functools
import math
import jax
import jax.numpy as jnp
from jax import lax
from jax.experimental import pallas as pl
from jax.experimental.pallas import tpu as pltpu
from jax.sharding import PartitionSpec as P

sharpness_divisor = 0.2
loss_scale = 4096.0
bn_eps = 1e-05
norm_eps = 1e-06
EXP2_SCALE = math.log2(math.e) / sharpness_divisor


MESH = pl.DeviceIdType.MESH
CHUNK = 16
LANES = 128
TURNS = (("x", 1), ("y", 1), ("z", 1), ("x", 3), ("y", 3), ("z", 3))
BLOCK = 1024
WIDE = 4
AXES = ("x", "y", "z")


def place():
    dp, crop = lax.axis_index("dp"), lax.axis_index("crop")
    return {
        "x": dp // 8,
        "z": (dp // 2) % 4,
        "y": (dp % 2) * 2 + crop // 2,
        "core": crop % 2,
    }


def device_of(at):
    return (at["x"] * 8 + at["z"] * 2 + at["y"] // 2, (at["y"] % 2) * 2 + at["core"])


def mirrored(v, u):
    return (v, v + 1 - 2 * (v % 2), (v + 2) % 4, 3 - v)[u]


def partner(at, turn):
    if turn is None:
        return device_of({**at, "core": 1 - at["core"]})
    axis, flip = turn
    return device_of({**at, axis: mirrored(at[axis], flip)})


def greet(at):
    barrier = pltpu.get_barrier_semaphore()
    for turn in (None,) + TURNS:
        pl.semaphore_signal(barrier, inc=1, device_id=partner(at, turn), device_id_type=MESH)
    pl.semaphore_wait(barrier, 1 + len(TURNS))


def plan_of(kind):
    held = {a: [0, 1, 2, 3] for a in AXES}
    hops = []
    for k in range(6):
        axis, flip = TURNS[(kind + k) % 6]
        now = held[axis]
        if len(now) == 4:
            sent = [1, 2] if flip == 1 else [3, 2]
        else:
            sent = [flip]
        kept = [u ^ flip for u in sent]
        dims = tuple(len(held[a]) for a in AXES)
        hops.append(
            (dims, AXES.index(axis), [now.index(u) for u in kept], [now.index(u) for u in sent])
        )
        held[axis] = kept
    return hops


PLANS = [plan_of(kind) for kind in range(6)]


def order_of(tiles, wide):
    steps, waiting = [("outer", None)], [tiles, tiles + 1]
    first = waiting + list(range(tiles))
    for g in range(tiles // wide):
        steps.append(("block", g))
        steps += [("hop", 0, t) for t in waiting]
        waiting = list(range(g * wide, (g + 1) * wide))
    steps += [("hop", 0, t) for t in waiting]
    return steps + [("hop", k, t) for k in range(1, 7) for t in first]


def grads_kernel(tiles, xt_ref, dh_ref, go_ref, gi_out, go_out, xp, *rest):
    acc, send, recv = rest[0:7], rest[7:14], rest[14:21]
    send_sem, recv_sem = rest[21], rest[22]
    slots = tiles + 2
    at = place()
    greet(at)

    def copy(k, t, kind):
        turn = None if k == 0 else TURNS[(kind + k - 1) % 6]
        return pltpu.make_async_remote_copy(
            src_ref=send[k].at[t],
            dst_ref=recv[k].at[t],
            send_sem=send_sem.at[k, t],
            recv_sem=recv_sem.at[k, t],
            device_id=partner(at, turn),
            device_id_type=MESH,
        )

    def combine(k, t, kind):
        copy(k, t, kind).wait_recv()
        total = acc[k][t] + recv[k][t].astype(jnp.float32)
        if k == 6:
            return total[0]
        dims, axis, kept, sent = PLANS[kind][k]
        total = total.reshape(dims + (CHUNK, LANES))
        out_dims = tuple(n // 2 if i == axis else n for i, n in enumerate(dims))

        def pick(positions):
            parts = [lax.slice_in_dim(total, p, p + 1, axis=axis) for p in positions]
            joined = parts[0] if len(parts) == 1 else jnp.concatenate(parts, axis=axis)
            return joined.reshape((-1, CHUNK, LANES))

        send[k + 1][t] = pick(sent).astype(jnp.bfloat16)
        acc[k + 1][t] = pick(kept)
        copy(k + 1, t, kind).start()

    rows = {}
    index = 0
    for far in (1, 0):
        core = at["core"] if far == 0 else 1 - at["core"]
        for ux in range(4):
            for uy in range(4):
                for uz in range(4):
                    wx, wy, wz = (mirrored(at[a], u) for a, u in zip(AXES, (ux, uy, uz)))
                    row = pl.multiple_of((((wx * 4 + wz) * 4 + wy) * 2 + core) * CHUNK, CHUNK)
                    rows[index] = row
                    xp[index * CHUNK : (index + 1) * CHUNK, :] = xt_ref[pl.ds(row, CHUNK), :]
                    index += 1

    def outer():
        for i in range(64):
            send[0][tiles, i] = go_ref[pl.ds(rows[i], CHUNK), :].astype(jnp.bfloat16)
            acc[0][tiles, i] = go_ref[pl.ds(rows[64 + i], CHUNK), :]
        send[0][tiles + 1] = jnp.zeros((64, CHUNK, LANES), jnp.bfloat16)
        acc[0][tiles + 1] = jnp.zeros((64, CHUNK, LANES), jnp.float32)
        for t in (tiles, tiles + 1):
            copy(0, t, t % 6).start()

    def inner(g):
        right = dh_ref[:, WIDE * g * LANES : (g + 1) * WIDE * LANES]

        def block(far, b):
            size = BLOCK // CHUNK
            first = pl.multiple_of(far * 1024 + b * BLOCK, BLOCK)
            left = xp[pl.ds(first, BLOCK), :]
            part = jnp.dot(left, right, preferred_element_type=jnp.float32)
            for h in range(WIDE):
                half = part[:, h * LANES : (h + 1) * LANES].reshape(size, CHUNK, LANES)
                where = pl.ds(b * size, size)
                if far == 0:
                    send[0][WIDE * g + h, where] = half.astype(jnp.bfloat16)
                else:
                    acc[0][WIDE * g + h, where] = half

        for far in (0, 1):
            if BLOCK == 1024:
                block(far, 0)
            else:

                @pl.loop(0, 1024 // BLOCK)
                def _(b, far=far):
                    block(far, b)

            if far == 0:
                for t in range(WIDE * g, WIDE * (g + 1)):
                    copy(0, t, t % 6).start()

    for step in order_of(tiles, WIDE):
        if step[0] == "outer":
            outer()
        elif step[0] == "block":
            inner(step[1])
        else:
            _, k, t = step
            done = combine(k, t, t % 6)
            if k == 6 and t < tiles:
                gi_out[:, t * LANES : (t + 1) * LANES] = done
            elif k == 6 and t == tiles:
                go_out[...] = done

    for k in range(7):

        @pl.loop(0, slots // 6)
        def _(r, k=k):
            for kind in range(6):
                copy(k, r * 6 + kind, kind).wait_send()


def summed_grads(crops_t, d_hidden, grad_outer):
    depth, batch = crops_t.shape
    width = d_hidden.shape[1]
    tiles = width // LANES
    slots = tiles + 2

    def slabs(dtype):
        return [pltpu.VMEM((slots, 64 >> k, CHUNK, LANES), dtype) for k in range(7)]

    return pl.pallas_call(
        functools.partial(grads_kernel, tiles),
        out_shape=(
            jax.ShapeDtypeStruct((CHUNK, width), jnp.float32),
            jax.ShapeDtypeStruct((CHUNK, LANES), jnp.float32),
        ),
        in_specs=[pl.BlockSpec(memory_space=pltpu.VMEM)] * 3,
        out_specs=[pl.BlockSpec(memory_space=pltpu.VMEM)] * 2,
        scratch_shapes=[pltpu.VMEM((depth, batch), jnp.bfloat16)]
        + slabs(jnp.float32)
        + [pltpu.VMEM((slots, 64, CHUNK, LANES), jnp.bfloat16)]
        + slabs(jnp.bfloat16)[1:]
        + slabs(jnp.bfloat16)
        + [pltpu.SemaphoreType.DMA((7, slots)), pltpu.SemaphoreType.DMA((7, slots))],
        compiler_params=pltpu.CompilerParams(
            collective_id=0, has_side_effects=True, vmem_limit_bytes=60 << 20
        ),
    )(crops_t, d_hidden, grad_outer)


def wanted_kernel(order_ref, out_ref, table, keep_sem, send_sem, recv_sem):
    at = place()
    barrier = pltpu.get_barrier_semaphore()
    others = [device_of({**at, "core": 1 - at["core"]})]
    for axis in AXES:
        others += [device_of({**at, axis: mirrored(at[axis], u)}) for u in (1, 2, 3)]
    for other in others:
        pl.semaphore_signal(barrier, inc=1, device_id=other, device_id_type=MESH)
    pl.semaphore_wait(barrier, len(others))

    mine = at["x"] * 32 + at["z"] * 8 + at["y"] * 2 + at["core"]
    keep = pltpu.make_async_copy(order_ref, table.at[:, mine], keep_sem.at[0])
    keep.start()
    keep.wait()

    def swap(phase, first, count, targets, sources=None):
        copies = []
        for i, target in enumerate(targets):
            if sources is None:
                part = (slice(None), pl.ds(first, count))
                source, landing = table.at[part], table.at[part]
            else:
                source = table.at[sources[i], pl.ds(first, count)]
                landing = out_ref.at[pl.ds(first, count)]
            copies.append(
                pltpu.make_async_remote_copy(
                    src_ref=source,
                    dst_ref=landing,
                    send_sem=send_sem.at[phase, i],
                    recv_sem=recv_sem.at[phase, i],
                    device_id=target,
                    device_id_type=MESH,
                )
            )
        for copy in copies:
            copy.start()
        return copies

    def finish(copies):
        for copy in copies:
            copy.wait()

    finish(swap(0, mine, 1, others[0:1]))
    finish(swap(1, mine - mine % 2, 2, others[4:7]))
    finish(swap(2, mine - mine % 8, 8, others[7:10]))
    block = at["x"] * 32
    own = pltpu.make_async_copy(
        table.at[at["x"], pl.ds(block, 32)], out_ref.at[pl.ds(block, 32)], keep_sem.at[1]
    )
    own.start()
    rows = [mirrored(at["x"], u) for u in (1, 2, 3)]
    finish(swap(3, block, 32, others[1:4], rows))
    own.wait()


def wanted_rows(shuffle):
    return pl.pallas_call(
        wanted_kernel,
        out_shape=jax.ShapeDtypeStruct((128, 1, LANES), jnp.int32),
        in_specs=[pl.BlockSpec(memory_space=pltpu.VMEM)],
        out_specs=pl.BlockSpec(memory_space=pltpu.VMEM),
        scratch_shapes=[
            pltpu.VMEM((4, 128, 1, LANES), jnp.int32),
            pltpu.SemaphoreType.DMA((2,)),
            pltpu.SemaphoreType.DMA((4, 3)),
            pltpu.SemaphoreType.DMA((4, 3)),
        ],
        compiler_params=pltpu.CompilerParams(collective_id=1, has_side_effects=True),
    )(shuffle.reshape(4, 1, LANES))


def negatives_kernel(chunk, q_ref, bank_ref, total_ref, pull_ref):
    @pl.when(pl.program_id(0) == 0)
    def _():
        total_ref[...] = jnp.zeros_like(total_ref)
        pull_ref[...] = jnp.zeros_like(pull_ref)

    keys = bank_ref[...]
    for start in range(0, q_ref.shape[0], chunk):
        rows = slice(start, start + chunk)
        sims = lax.dot_general(
            q_ref[rows, :].astype(jnp.bfloat16), keys, (((1,), (1,)), ((), ())), preferred_element_type=jnp.float32
        )
        quarter = jnp.exp2(sims * EXP2_SCALE - 2.0)
        partial = quarter[:, 0:LANES]
        for c in range(LANES, quarter.shape[1], LANES):
            partial = partial + quarter[:, c : c + LANES]
        total_ref[rows, :] += partial
        pull_ref[rows, :] += jnp.dot(
            quarter.astype(jnp.bfloat16), keys, preferred_element_type=jnp.float32
        )


def negatives(probe_features, distractor_bank, block=4096, chunk=256):
    rows, emb = probe_features.shape
    keys = distractor_bank.shape[0]
    whole = pl.BlockSpec((rows, emb), lambda i: (0, 0))
    return pl.pallas_call(
        functools.partial(negatives_kernel, chunk),
        grid=(keys // block,),
        out_shape=(jax.ShapeDtypeStruct((rows, emb), jnp.float32),) * 2,
        in_specs=[whole, pl.BlockSpec((block, emb), lambda i: (i, 0))],
        out_specs=[whole, whole],
        cost_estimate=pl.CostEstimate(
            flops=4 * rows * keys * emb, bytes_accessed=2 * keys * emb, transcendentals=rows * keys
        ),
        compiler_params=pltpu.CompilerParams(vmem_limit_bytes=60 << 20),
    )(probe_features, distractor_bank)


def batch_stats(hidden):
    average = jnp.mean(hidden, axis=0)
    variance = jnp.mean(hidden * hidden, axis=0) - average * average
    return (average, lax.rsqrt(variance + bn_eps))


def head_tail(normed, w_out):
    active = jnp.maximum(normed, 0.0).astype(jnp.bfloat16)
    projected = jnp.dot(active, w_out, preferred_element_type=jnp.float32)
    return projected * lax.rsqrt(jnp.sum(projected * projected, axis=-1, keepdims=True) + norm_eps)


def key_embed(crop_rows, w_in, w_out):
    hidden = jnp.dot(crop_rows, w_in, preferred_element_type=jnp.float32)
    average, inv_std = batch_stats(hidden)
    return head_tail((hidden - average) * inv_std, w_out)


def query_forward(crop_rows, w_in, w_out):
    hidden = jnp.dot(crop_rows, w_in, preferred_element_type=jnp.float32)
    average, inv_std = batch_stats(hidden)
    normed = (hidden - average) * inv_std
    active = jnp.maximum(normed, 0.0).astype(jnp.bfloat16)
    projected = jnp.dot(active, w_out, preferred_element_type=jnp.float32)
    inv_len = lax.rsqrt(jnp.sum(projected * projected, axis=-1, keepdims=True) + norm_eps)
    return (normed, active, inv_std, inv_len, projected * inv_len)


def query_grads(crops_t, forward, lane_totals, pull, matching_targets, w_out, all_rows):
    normed, active, inv_std, inv_len, probe_features = forward
    matching_similarity = (
        jnp.sum(probe_features * matching_targets, axis=-1, keepdims=True) / sharpness_divisor
    )
    exp_pos = jnp.exp(matching_similarity) * 0.25
    total_exp = exp_pos + jnp.sum(lane_totals, axis=-1, keepdims=True)
    scale_coef = loss_scale / all_rows
    matching_similarity_slope = scale_coef * (exp_pos / total_exp - 1.0)
    probe_feature_slope = (
        matching_similarity_slope * matching_targets + scale_coef * pull / total_exp
    ) / sharpness_divisor
    d_proj = (
        (
            probe_feature_slope
            - probe_features * jnp.sum(probe_feature_slope * probe_features, axis=-1, keepdims=True)
        )
        * inv_len
    ).astype(jnp.bfloat16)
    grad_out = lax.dot_general(
        active, d_proj, (((0,), (0,)), ((), ())), preferred_element_type=jnp.float32
    )
    d_act = lax.dot_general(
        d_proj, w_out, (((1,), (1,)), ((), ())), preferred_element_type=jnp.float32
    )
    d_norm = jnp.where(normed > 0.0, d_act, 0.0)
    d_hidden = inv_std * (
        d_norm - jnp.mean(d_norm, axis=0) - normed * jnp.mean(d_norm * normed, axis=0)
    )
    return summed_grads(crops_t, d_hidden.astype(jnp.bfloat16), grad_out)


def per_device(
    query_crops, key_crops, shuffle, distractor_bank, query_inner, query_outer, key_inner, key_outer
):
    group_count = lax.axis_size(("dp", "crop"))
    row_count = query_crops.shape[0]
    per_peer = row_count // group_count
    all_rows = float(row_count * group_count)
    lane = (lax.axis_index(("dp", "crop")) % 32) * per_peer
    requested = lax.dynamic_slice_in_dim(
        wanted_rows(shuffle).reshape(group_count, LANES), lane, per_peer, axis=1
    )
    flat_req = requested.reshape(-1) % row_count
    outgoing = key_crops[flat_req].reshape(group_count, per_peer, key_crops.shape[1])
    incoming = lax.all_to_all(outgoing, ("dp", "crop"), split_axis=0, concat_axis=0, tiled=True)
    forward = query_forward(query_crops, query_inner, query_outer)
    crops_t = query_crops.T
    lane_totals, pull = negatives(forward[4], distractor_bank)
    incoming, lane_totals, pull, crops_t = lax.optimization_barrier(
        (incoming, lane_totals, pull, crops_t)
    )
    embedded = key_embed(
        incoming.reshape(row_count, key_crops.shape[1]), key_inner, key_outer
    ).reshape(group_count, per_peer, key_outer.shape[1])
    returned = lax.all_to_all(
        embedded, ("dp", "crop"), split_axis=0, concat_axis=0, tiled=True
    ).reshape(row_count, key_outer.shape[1])
    matching_targets = (
        jnp.zeros((row_count, returned.shape[1]), jnp.float32).at[flat_req].set(returned)
    )
    return query_grads(
        crops_t, forward, lane_totals, pull, matching_targets, query_outer, all_rows
    )


def solution(mesh):
    placed = (
        P(("dp", "crop"), None),
        P(("dp", "crop"), None),
        P(("dp", "crop")),
        P(),
        P(),
        P(),
        P(),
        P(),
    )
    return jax.shard_map(
        per_device,
        mesh=mesh,
        in_specs=placed,
        out_specs=(P(("dp", "crop"), None), P(("dp", "crop"), None)),
        check_vma=False,
    )
```

```python
import functools
import math
import jax
import jax.numpy as jnp
from jax import lax
from jax.experimental import pallas as pl
from jax.experimental.pallas import tpu as pltpu
from jax.sharding import PartitionSpec as P

sharpness_divisor = 0.2
loss_scale = 4096.0
bn_eps = 1e-05
norm_eps = 1e-06
EXP2_SCALE = math.log2(math.e) / sharpness_divisor


MESH = pl.DeviceIdType.MESH
CHUNK = 16
LANES = 128
TURNS = (("x", 1), ("y", 1), ("z", 1), ("x", 3), ("y", 3), ("z", 3))
BLOCK = 1024
WIDE = 4
AXES = ("x", "y", "z")


def place():
    dp, crop = lax.axis_index("dp"), lax.axis_index("crop")
    return {
        "x": dp // 8,
        "z": (dp // 2) % 4,
        "y": (dp % 2) * 2 + crop // 2,
        "core": crop % 2,
    }


def device_of(at):
    return (at["x"] * 8 + at["z"] * 2 + at["y"] // 2, (at["y"] % 2) * 2 + at["core"])


def mirrored(v, u):
    return (v, v + 1 - 2 * (v % 2), (v + 2) % 4, 3 - v)[u]


def partner(at, turn):
    if turn is None:
        return device_of({**at, "core": 1 - at["core"]})
    axis, flip = turn
    return device_of({**at, axis: mirrored(at[axis], flip)})


def plan_of(kind):
    held = {a: [0, 1, 2, 3] for a in AXES}
    hops = []
    for k in range(6):
        axis, flip = TURNS[(kind + k) % 6]
        now = held[axis]
        if len(now) == 4:
            sent = [1, 2] if flip == 1 else [3, 2]
        else:
            sent = [flip]
        kept = [u ^ flip for u in sent]
        dims = tuple(len(held[a]) for a in AXES)
        hops.append(
            (dims, AXES.index(axis), [now.index(u) for u in kept], [now.index(u) for u in sent])
        )
        held[axis] = kept
    return hops


PLANS = [plan_of(kind) for kind in range(6)]


def order_of(tiles, wide):
    steps, waiting = [("outer", None)], [tiles, tiles + 1]
    first = waiting + list(range(tiles))
    for g in range(tiles // wide):
        steps.append(("block", g))
        steps += [("hop", 0, t) for t in waiting]
        waiting = list(range(g * wide, (g + 1) * wide))
    steps += [("hop", 0, t) for t in waiting]
    return steps + [("hop", k, t) for k in range(1, 7) for t in first]


def grads_kernel(
    tiles, xt_ref, hid_ref, stats_ref, dz_ref, w_ref, go_ref, out_ref, xp, slope, *rest
):
    acc, send, recv = rest[0:7], rest[7:14], rest[14:21]
    send_sem, recv_sem = rest[21], rest[22]
    slots = tiles + 2
    at = place()
    barrier = pltpu.get_barrier_semaphore()
    for turn in (None,) + TURNS:
        pl.semaphore_signal(barrier, inc=1, device_id=partner(at, turn), device_id_type=MESH)

    def copy(k, t, kind):
        turn = None if k == 0 else TURNS[(kind + k - 1) % 6]
        return pltpu.make_async_remote_copy(
            src_ref=send[k].at[t],
            dst_ref=recv[k].at[t],
            send_sem=send_sem.at[k, t],
            recv_sem=recv_sem.at[k, t],
            device_id=partner(at, turn),
            device_id_type=MESH,
        )

    def combine(k, t, kind):
        copy(k, t, kind).wait_recv()
        total = acc[k][t] + recv[k][t].astype(jnp.float32)
        if k == 6:
            return total[0]
        dims, axis, kept, sent = PLANS[kind][k]
        total = total.reshape(dims + (CHUNK, LANES))
        out_dims = tuple(n // 2 if i == axis else n for i, n in enumerate(dims))

        def pick(positions):
            parts = [lax.slice_in_dim(total, p, p + 1, axis=axis) for p in positions]
            joined = parts[0] if len(parts) == 1 else jnp.concatenate(parts, axis=axis)
            return joined.reshape((-1, CHUNK, LANES))

        send[k + 1][t] = pick(sent).astype(jnp.bfloat16)
        acc[k + 1][t] = pick(kept)
        copy(k + 1, t, kind).start()

    rows = {}
    index = 0
    for far in (1, 0):
        core = at["core"] if far == 0 else 1 - at["core"]
        for ux in range(4):
            for uy in range(4):
                for uz in range(4):
                    wx, wy, wz = (mirrored(at[a], u) for a, u in zip(AXES, (ux, uy, uz)))
                    row = pl.multiple_of((((wx * 4 + wz) * 4 + wy) * 2 + core) * CHUNK, CHUNK)
                    rows[index] = row
                    xp[index * CHUNK : (index + 1) * CHUNK, :] = xt_ref[pl.ds(row, CHUNK), :]
                    index += 1

    def outer():
        for i in range(64):
            send[0][tiles, i] = go_ref[pl.ds(rows[i], CHUNK), :].astype(jnp.bfloat16)
            acc[0][tiles, i] = go_ref[pl.ds(rows[64 + i], CHUNK), :]
        send[0][tiles + 1] = jnp.zeros((64, CHUNK, LANES), jnp.bfloat16)
        acc[0][tiles + 1] = jnp.zeros((64, CHUNK, LANES), jnp.float32)
        pl.semaphore_wait(barrier, 1 + len(TURNS))
        for t in (tiles, tiles + 1):
            copy(0, t, t % 6).start()

    def inner(g):
        cols = slice(WIDE * g * LANES, (g + 1) * WIDE * LANES)
        inv_std = stats_ref[1:2, cols]
        normed = (hid_ref[:, cols] - stats_ref[0:1, cols]) * inv_std
        d_act = lax.dot_general(
            dz_ref[...], w_ref[cols, :], (((1,), (1,)), ((), ())), preferred_element_type=jnp.float32
        )
        d_norm = jnp.where(normed > 0.0, d_act, 0.0)
        d_mean = jnp.mean(d_norm, axis=0, keepdims=True)
        d_pull = jnp.mean(d_norm * normed, axis=0, keepdims=True)
        slope[g % 2] = (inv_std * (d_norm - d_mean - normed * d_pull)).astype(jnp.bfloat16)
        right = slope[g % 2]

        def block(far, b):
            size = BLOCK // CHUNK
            first = pl.multiple_of(far * 1024 + b * BLOCK, BLOCK)
            left = xp[pl.ds(first, BLOCK), :]
            part = jnp.dot(left, right, preferred_element_type=jnp.float32)
            for h in range(WIDE):
                half = part[:, h * LANES : (h + 1) * LANES].reshape(size, CHUNK, LANES)
                where = pl.ds(b * size, size)
                if far == 0:
                    send[0][WIDE * g + h, where] = half.astype(jnp.bfloat16)
                else:
                    acc[0][WIDE * g + h, where] = half

        for far in (0, 1):
            if BLOCK == 1024:
                block(far, 0)
            else:

                @pl.loop(0, 1024 // BLOCK)
                def _(b, far=far):
                    block(far, b)

            if far == 0:
                for t in range(WIDE * g, WIDE * (g + 1)):
                    copy(0, t, t % 6).start()

    for step in order_of(tiles, WIDE):
        if step[0] == "outer":
            outer()
        elif step[0] == "block":
            inner(step[1])
        else:
            _, k, t = step
            done = combine(k, t, t % 6)
            if k == 6 and t <= tiles:
                out_ref[:, t * LANES : (t + 1) * LANES] = done

    for k in range(7):

        @pl.loop(0, slots // 6)
        def _(r, k=k):
            for kind in range(6):
                copy(k, r * 6 + kind, kind).wait_send()


def summed_grads(crops_t, hidden, stats, d_proj, w_out, grad_outer):
    depth, batch = crops_t.shape
    width = hidden.shape[1]
    tiles = width // LANES
    slots = tiles + 2

    def slabs(dtype):
        return [pltpu.VMEM((slots, 64 >> k, CHUNK, LANES), dtype) for k in range(7)]

    summed = pl.pallas_call(
        functools.partial(grads_kernel, tiles),
        out_shape=jax.ShapeDtypeStruct((CHUNK, width + LANES), jnp.float32),
        in_specs=[pl.BlockSpec(memory_space=pltpu.VMEM)] * 6,
        out_specs=pl.BlockSpec(memory_space=pltpu.VMEM),
        scratch_shapes=[
            pltpu.VMEM((depth, batch), jnp.bfloat16),
            pltpu.VMEM((2, batch, WIDE * LANES), jnp.bfloat16),
        ]
        + slabs(jnp.float32)
        + slabs(jnp.bfloat16)
        + slabs(jnp.bfloat16)
        + [pltpu.SemaphoreType.DMA((7, slots)), pltpu.SemaphoreType.DMA((7, slots))],
        compiler_params=pltpu.CompilerParams(
            collective_id=0, has_side_effects=True, vmem_limit_bytes=56 << 20
        ),
    )(crops_t, hidden, stats, d_proj, w_out, grad_outer)
    return (summed[:, :width], summed[:, width:])


def wanted_kernel(order_ref, out_ref, table, keep_sem, send_sem, recv_sem):
    at = place()
    barrier = pltpu.get_barrier_semaphore()
    others = [device_of({**at, "core": 1 - at["core"]})]
    for axis in AXES:
        others += [device_of({**at, axis: mirrored(at[axis], u)}) for u in (1, 2, 3)]
    for other in others:
        pl.semaphore_signal(barrier, inc=1, device_id=other, device_id_type=MESH)
    pl.semaphore_wait(barrier, len(others))

    mine = at["x"] * 32 + at["z"] * 8 + at["y"] * 2 + at["core"]
    keep = pltpu.make_async_copy(order_ref, table.at[:, mine], keep_sem.at[0])
    keep.start()
    keep.wait()

    def swap(phase, first, count, targets, sources=None):
        copies = []
        for i, target in enumerate(targets):
            if sources is None:
                part = (slice(None), pl.ds(first, count))
                source, landing = table.at[part], table.at[part]
            else:
                source = table.at[sources[i], pl.ds(first, count)]
                landing = out_ref.at[pl.ds(first, count)]
            copies.append(
                pltpu.make_async_remote_copy(
                    src_ref=source,
                    dst_ref=landing,
                    send_sem=send_sem.at[phase, i],
                    recv_sem=recv_sem.at[phase, i],
                    device_id=target,
                    device_id_type=MESH,
                )
            )
        for copy in copies:
            copy.start()
        return copies

    def finish(copies):
        for copy in copies:
            copy.wait()

    finish(swap(0, mine, 1, others[0:1]))
    finish(swap(1, mine - mine % 2, 2, others[4:7]))
    finish(swap(2, mine - mine % 8, 8, others[7:10]))
    block = at["x"] * 32
    own = pltpu.make_async_copy(
        table.at[at["x"], pl.ds(block, 32)], out_ref.at[pl.ds(block, 32)], keep_sem.at[1]
    )
    own.start()
    rows = [mirrored(at["x"], u) for u in (1, 2, 3)]
    finish(swap(3, block, 32, others[1:4], rows))
    own.wait()


def wanted_rows(shuffle):
    return pl.pallas_call(
        wanted_kernel,
        out_shape=jax.ShapeDtypeStruct((128, 1, LANES), jnp.int32),
        in_specs=[pl.BlockSpec(memory_space=pltpu.VMEM)],
        out_specs=pl.BlockSpec(memory_space=pltpu.VMEM),
        scratch_shapes=[
            pltpu.VMEM((4, 128, 1, LANES), jnp.int32),
            pltpu.SemaphoreType.DMA((2,)),
            pltpu.SemaphoreType.DMA((4, 3)),
            pltpu.SemaphoreType.DMA((4, 3)),
        ],
        compiler_params=pltpu.CompilerParams(collective_id=1, has_side_effects=True),
    )(shuffle.reshape(4, 1, LANES))


def negatives_kernel(chunk, q_ref, bank_ref, total_ref, pull_ref):
    @pl.when(pl.program_id(0) == 0)
    def _():
        total_ref[...] = jnp.zeros_like(total_ref)
        pull_ref[...] = jnp.zeros_like(pull_ref)

    keys = bank_ref[...]
    for start in range(0, q_ref.shape[0], chunk):
        rows = slice(start, start + chunk)
        sims = lax.dot_general(
            q_ref[rows, :].astype(jnp.bfloat16), keys, (((1,), (1,)), ((), ())), preferred_element_type=jnp.float32
        )
        quarter = jnp.exp2(sims * EXP2_SCALE - 2.0)
        partial = quarter[:, 0:LANES]
        for c in range(LANES, quarter.shape[1], LANES):
            partial = partial + quarter[:, c : c + LANES]
        total_ref[rows, :] += partial
        pull_ref[rows, :] += jnp.dot(
            quarter.astype(jnp.bfloat16), keys, preferred_element_type=jnp.float32
        )


def negatives(probe_features, distractor_bank, block=4096, chunk=256):
    rows, emb = probe_features.shape
    keys = distractor_bank.shape[0]
    whole = pl.BlockSpec((rows, emb), lambda i: (0, 0))
    return pl.pallas_call(
        functools.partial(negatives_kernel, chunk),
        grid=(keys // block,),
        out_shape=(jax.ShapeDtypeStruct((rows, emb), jnp.float32),) * 2,
        in_specs=[whole, pl.BlockSpec((block, emb), lambda i: (i, 0))],
        out_specs=[whole, whole],
        cost_estimate=pl.CostEstimate(
            flops=4 * rows * keys * emb, bytes_accessed=2 * keys * emb, transcendentals=rows * keys
        ),
        compiler_params=pltpu.CompilerParams(vmem_limit_bytes=24 << 20),
    )(probe_features, distractor_bank)


def batch_stats(hidden):
    average = jnp.mean(hidden, axis=0)
    variance = jnp.mean(hidden * hidden, axis=0) - average * average
    return (average, lax.rsqrt(variance + bn_eps))


def head_tail(normed, w_out):
    active = jnp.maximum(normed, 0.0).astype(jnp.bfloat16)
    projected = jnp.einsum("gjh,he->gje", active, w_out, preferred_element_type=jnp.float32)
    return projected * lax.rsqrt(jnp.sum(projected * projected, axis=-1, keepdims=True) + norm_eps)


def key_embed(crop_rows, w_in, w_out):
    hidden = jnp.einsum("gjd,dh->gjh", crop_rows, w_in, preferred_element_type=jnp.float32)
    average = jnp.mean(hidden, axis=(0, 1))
    variance = jnp.mean(hidden * hidden, axis=(0, 1)) - average * average
    return head_tail((hidden - average) * lax.rsqrt(variance + bn_eps), w_out)


def query_forward(crop_rows, w_in, w_out):
    hidden = jnp.dot(crop_rows, w_in, preferred_element_type=jnp.float32)
    average, inv_std = batch_stats(hidden)
    normed = (hidden - average) * inv_std
    active = jnp.maximum(normed, 0.0).astype(jnp.bfloat16)
    projected = jnp.dot(active, w_out, preferred_element_type=jnp.float32)
    inv_len = lax.rsqrt(jnp.sum(projected * projected, axis=-1, keepdims=True) + norm_eps)
    stats = jnp.stack([average, inv_std])
    return (hidden, stats, active, inv_len, projected * inv_len)


def query_grads(crops_t, forward, lane_totals, pull, matching_targets, w_out, all_rows):
    hidden, stats, active, inv_len, probe_features = forward
    matching_similarity = (
        jnp.sum(probe_features * matching_targets, axis=-1, keepdims=True) / sharpness_divisor
    )
    exp_pos = jnp.exp(matching_similarity) * 0.25
    total_exp = exp_pos + jnp.sum(lane_totals, axis=-1, keepdims=True)
    scale_coef = loss_scale / all_rows
    matching_similarity_slope = scale_coef * (exp_pos / total_exp - 1.0)
    probe_feature_slope = (
        matching_similarity_slope * matching_targets + scale_coef * pull / total_exp
    ) / sharpness_divisor
    d_proj = (
        (
            probe_feature_slope
            - probe_features * jnp.sum(probe_feature_slope * probe_features, axis=-1, keepdims=True)
        )
        * inv_len
    ).astype(jnp.bfloat16)
    grad_out = lax.dot_general(
        active, d_proj, (((0,), (0,)), ((), ())), preferred_element_type=jnp.float32
    )
    return summed_grads(crops_t, hidden, stats, d_proj, w_out, grad_out)


def per_device(
    query_crops, key_crops, shuffle, distractor_bank, query_inner, query_outer, key_inner, key_outer
):
    group_count = lax.axis_size(("dp", "crop"))
    row_count = query_crops.shape[0]
    per_peer = row_count // group_count
    all_rows = float(row_count * group_count)
    lane = (lax.axis_index(("dp", "crop")) % 32) * per_peer
    requested = lax.dynamic_slice_in_dim(
        wanted_rows(shuffle).reshape(group_count, LANES), lane, per_peer, axis=1
    )
    flat_req = requested.reshape(-1) % row_count
    outgoing = key_crops[flat_req].reshape(group_count, per_peer, key_crops.shape[1])
    incoming = lax.all_to_all(outgoing, ("dp", "crop"), split_axis=0, concat_axis=0, tiled=True)
    forward = query_forward(query_crops, query_inner, query_outer)
    crops_t = query_crops.T
    lane_totals, pull = negatives(forward[4], distractor_bank)
    incoming, lane_totals, pull, crops_t = lax.optimization_barrier(
        (incoming, lane_totals, pull, crops_t)
    )
    embedded = key_embed(incoming, key_inner, key_outer)
    returned = lax.all_to_all(
        embedded, ("dp", "crop"), split_axis=0, concat_axis=0, tiled=True
    ).reshape(row_count, key_outer.shape[1])
    matching_targets = (
        jnp.zeros((row_count, returned.shape[1]), jnp.float32).at[flat_req].set(returned)
    )
    return query_grads(
        crops_t, forward, lane_totals, pull, matching_targets, query_outer, all_rows
    )


def solution(mesh):
    placed = (
        P(("dp", "crop"), None),
        P(("dp", "crop"), None),
        P(("dp", "crop")),
        P(),
        P(),
        P(),
        P(),
        P(),
    )
    return jax.shard_map(
        per_device,
        mesh=mesh,
        in_specs=placed,
        out_specs=(P(("dp", "crop"), None), P(("dp", "crop"), None)),
        check_vma=False,
    )
```

```python
import functools
import math
import jax
import jax.numpy as jnp
from jax import lax
from jax.experimental import pallas as pl
from jax.experimental.pallas import tpu as pltpu
from jax.sharding import PartitionSpec as P

sharpness_divisor = 0.2
loss_scale = 4096.0
bn_eps = 1e-05
norm_eps = 1e-06
EXP2_SCALE = math.log2(math.e) / sharpness_divisor


MESH = pl.DeviceIdType.MESH
CHUNK = 16
LANES = 128
TURNS = (("x", 1), ("y", 1), ("z", 1), ("x", 3), ("y", 3), ("z", 3))
BLOCK = 1024
WIDE = 4
AXES = ("x", "y", "z")


def place():
    dp, crop = lax.axis_index("dp"), lax.axis_index("crop")
    return {
        "x": dp // 8,
        "z": (dp // 2) % 4,
        "y": (dp % 2) * 2 + crop // 2,
        "core": crop % 2,
    }


def device_of(at):
    return (at["x"] * 8 + at["z"] * 2 + at["y"] // 2, (at["y"] % 2) * 2 + at["core"])


def mirrored(v, u):
    return (v, v + 1 - 2 * (v % 2), (v + 2) % 4, 3 - v)[u]


def partner(at, turn):
    if turn is None:
        return device_of({**at, "core": 1 - at["core"]})
    axis, flip = turn
    return device_of({**at, axis: mirrored(at[axis], flip)})


def plan_of(kind):
    held = {a: [0, 1, 2, 3] for a in AXES}
    hops = []
    for k in range(6):
        axis, flip = TURNS[(kind + k) % 6]
        now = held[axis]
        if len(now) == 4:
            sent = [1, 2] if flip == 1 else [3, 2]
        else:
            sent = [flip]
        kept = [u ^ flip for u in sent]
        dims = tuple(len(held[a]) for a in AXES)
        hops.append(
            (dims, AXES.index(axis), [now.index(u) for u in kept], [now.index(u) for u in sent])
        )
        held[axis] = kept
    return hops


PLANS = [plan_of(kind) for kind in range(6)]


def order_of(tiles, wide):
    steps, waiting = [], []
    first = list(range(tiles + 2))
    for g in range(tiles // wide):
        steps.append(("block", g))
        steps += [("hop", 0, t) for t in waiting]
        waiting = first[g * wide : (g + 1) * wide]
    steps.append(("outer", None))
    steps += [("hop", 0, t) for t in waiting + first[tiles:]]
    return steps + [("hop", k, t) for k in range(1, 7) for t in first]


def grads_kernel(
    tiles,
    xt_any,
    hid_any,
    stats_ref,
    dz_ref,
    w_ref,
    out_ref,
    xt_ref,
    hid_ref,
    go_ref,
    load_sem,
    xp,
    slope,
    *rest,
):
    acc, send, recv = rest[0:7], rest[7:14], rest[14:21]
    send_sem, recv_sem = rest[21], rest[22]
    slots = tiles + 2
    at = place()
    barrier = pltpu.get_barrier_semaphore()
    for turn in (None,) + TURNS:
        pl.semaphore_signal(barrier, inc=1, device_id=partner(at, turn), device_id_type=MESH)

    def columns(g):
        return slice(WIDE * g * LANES, (g + 1) * WIDE * LANES)

    blocks = tiles // WIDE
    loads = [
        pltpu.make_async_copy(hid_any.at[:, columns(g)], hid_ref.at[g], load_sem.at[g])
        for g in range(blocks)
    ]
    loads.append(pltpu.make_async_copy(xt_any, xt_ref, load_sem.at[blocks]))
    for i in (blocks, *range(blocks)):
        loads[i].start()
    loads[blocks].wait()

    def copy(k, t, kind):
        turn = None if k == 0 else TURNS[(kind + k - 1) % 6]
        return pltpu.make_async_remote_copy(
            src_ref=send[k].at[t],
            dst_ref=recv[k].at[t],
            send_sem=send_sem.at[k, t],
            recv_sem=recv_sem.at[k, t],
            device_id=partner(at, turn),
            device_id_type=MESH,
        )

    def combine(k, t, kind):
        copy(k, t, kind).wait_recv()
        total = acc[k][t] + recv[k][t].astype(jnp.float32)
        if k == 6:
            return total[0]
        dims, axis, kept, sent = PLANS[kind][k]
        total = total.reshape(dims + (CHUNK, LANES))
        out_dims = tuple(n // 2 if i == axis else n for i, n in enumerate(dims))

        def pick(positions):
            parts = [lax.slice_in_dim(total, p, p + 1, axis=axis) for p in positions]
            joined = parts[0] if len(parts) == 1 else jnp.concatenate(parts, axis=axis)
            return joined.reshape((-1, CHUNK, LANES))

        send[k + 1][t] = pick(sent).astype(jnp.bfloat16)
        acc[k + 1][t] = pick(kept)
        copy(k + 1, t, kind).start()

    rows = {}
    index = 0
    for far in (1, 0):
        core = at["core"] if far == 0 else 1 - at["core"]
        for ux in range(4):
            for uy in range(4):
                for uz in range(4):
                    wx, wy, wz = (mirrored(at[a], u) for a, u in zip(AXES, (ux, uy, uz)))
                    row = pl.multiple_of((((wx * 4 + wz) * 4 + wy) * 2 + core) * CHUNK, CHUNK)
                    rows[index] = row
                    xp[index * CHUNK : (index + 1) * CHUNK, :] = xt_ref[pl.ds(row, CHUNK), :]
                    index += 1

    def outer():
        for i in range(64):
            send[0][tiles, i] = go_ref[pl.ds(rows[i], CHUNK), :].astype(jnp.bfloat16)
            acc[0][tiles, i] = go_ref[pl.ds(rows[64 + i], CHUNK), :]
        send[0][tiles + 1] = jnp.zeros((64, CHUNK, LANES), jnp.bfloat16)
        acc[0][tiles + 1] = jnp.zeros((64, CHUNK, LANES), jnp.float32)
        for t in (tiles, tiles + 1):
            copy(0, t, t % 6).start()

    def inner(g):
        cols = columns(g)
        loads[g].wait()
        inv_std = stats_ref[1:2, cols]
        normed = (hid_ref[g] - stats_ref[0:1, cols]) * inv_std
        d_act = lax.dot_general(
            dz_ref[...], w_ref[cols, :], (((1,), (1,)), ((), ())), preferred_element_type=jnp.float32
        )
        d_norm = jnp.where(normed > 0.0, d_act, 0.0)
        d_mean = jnp.mean(d_norm, axis=0, keepdims=True)
        d_pull = jnp.mean(d_norm * normed, axis=0, keepdims=True)
        slope[g % 2] = (inv_std * (d_norm - d_mean - normed * d_pull)).astype(jnp.bfloat16)
        right = slope[g % 2]

        def block(far, b):
            size = BLOCK // CHUNK
            first = pl.multiple_of(far * 1024 + b * BLOCK, BLOCK)
            left = xp[pl.ds(first, BLOCK), :]
            part = jnp.dot(left, right, preferred_element_type=jnp.float32)
            for h in range(WIDE):
                half = part[:, h * LANES : (h + 1) * LANES].reshape(size, CHUNK, LANES)
                where = pl.ds(b * size, size)
                if far == 0:
                    send[0][WIDE * g + h, where] = half.astype(jnp.bfloat16)
                else:
                    acc[0][WIDE * g + h, where] = half

        for far in (0, 1):
            if BLOCK == 1024:
                block(far, 0)
            else:

                @pl.loop(0, 1024 // BLOCK)
                def _(b, far=far):
                    block(far, b)

            if far == 0:
                if g == 0:
                    pl.semaphore_wait(barrier, 1 + len(TURNS))
                for t in range(WIDE * g, WIDE * (g + 1)):
                    copy(0, t, t % 6).start()

        active = jnp.maximum(normed, 0.0).astype(jnp.bfloat16)
        turned = lax.dot_general(
            dz_ref[...], active, (((0,), (0,)), ((), ())), preferred_element_type=jnp.float32
        )
        go_ref[cols, :] = jnp.transpose(turned)

    for step in order_of(tiles, WIDE):
        if step[0] == "outer":
            outer()
        elif step[0] == "block":
            inner(step[1])
        else:
            _, k, t = step
            done = combine(k, t, t % 6)
            if k == 6 and t <= tiles:
                out_ref[:, t * LANES : (t + 1) * LANES] = done

    for k in range(7):

        @pl.loop(0, slots // 6)
        def _(r, k=k):
            for kind in range(6):
                copy(k, r * 6 + kind, kind).wait_send()


def summed_grads(crops_t, hidden, stats, d_proj, w_out):
    depth, batch = crops_t.shape
    width = hidden.shape[1]
    tiles = width // LANES
    slots = tiles + 2

    def slabs(dtype):
        return [pltpu.VMEM((slots, 64 >> k, CHUNK, LANES), dtype) for k in range(7)]

    summed = pl.pallas_call(
        functools.partial(grads_kernel, tiles),
        out_shape=jax.ShapeDtypeStruct((CHUNK, width + LANES), jnp.float32),
        in_specs=[pl.BlockSpec(memory_space=pl.ANY)] * 2
        + [pl.BlockSpec(memory_space=pltpu.VMEM)] * 3,
        out_specs=pl.BlockSpec(memory_space=pltpu.VMEM),
        scratch_shapes=[
            pltpu.VMEM((depth, batch), jnp.bfloat16),
            pltpu.VMEM((tiles // WIDE, batch, WIDE * LANES), jnp.float32),
            pltpu.VMEM((width, LANES), jnp.float32),
            pltpu.SemaphoreType.DMA((tiles // WIDE + 1,)),
            pltpu.VMEM((depth, batch), jnp.bfloat16),
            pltpu.VMEM((2, batch, WIDE * LANES), jnp.bfloat16),
        ]
        + slabs(jnp.float32)
        + slabs(jnp.bfloat16)
        + slabs(jnp.bfloat16)
        + [pltpu.SemaphoreType.DMA((7, slots)), pltpu.SemaphoreType.DMA((7, slots))],
        compiler_params=pltpu.CompilerParams(
            collective_id=0, has_side_effects=True, vmem_limit_bytes=56 << 20
        ),
    )(crops_t, hidden, stats, d_proj, w_out)
    return (summed[:, :width], summed[:, width:])


def wanted_kernel(order_ref, out_ref, table, keep_sem, send_sem, recv_sem):
    at = place()
    barrier = pltpu.get_barrier_semaphore()
    others = [device_of({**at, "core": 1 - at["core"]})]
    for axis in AXES:
        others += [device_of({**at, axis: mirrored(at[axis], u)}) for u in (1, 2, 3)]
    for other in others:
        pl.semaphore_signal(barrier, inc=1, device_id=other, device_id_type=MESH)
    pl.semaphore_wait(barrier, len(others))

    mine = at["x"] * 32 + at["z"] * 8 + at["y"] * 2 + at["core"]
    keep = pltpu.make_async_copy(order_ref, table.at[:, mine], keep_sem.at[0])
    keep.start()
    keep.wait()

    def swap(phase, first, count, targets, sources=None):
        copies = []
        for i, target in enumerate(targets):
            if sources is None:
                part = (slice(None), pl.ds(first, count))
                source, landing = table.at[part], table.at[part]
            else:
                source = table.at[sources[i], pl.ds(first, count)]
                landing = out_ref.at[pl.ds(first, count)]
            copies.append(
                pltpu.make_async_remote_copy(
                    src_ref=source,
                    dst_ref=landing,
                    send_sem=send_sem.at[phase, i],
                    recv_sem=recv_sem.at[phase, i],
                    device_id=target,
                    device_id_type=MESH,
                )
            )
        for copy in copies:
            copy.start()
        return copies

    def finish(copies):
        for copy in copies:
            copy.wait()

    finish(swap(0, mine, 1, others[0:1]))
    finish(swap(1, mine - mine % 2, 2, others[4:7]))
    finish(swap(2, mine - mine % 8, 8, others[7:10]))
    block = at["x"] * 32
    own = pltpu.make_async_copy(
        table.at[at["x"], pl.ds(block, 32)], out_ref.at[pl.ds(block, 32)], keep_sem.at[1]
    )
    own.start()
    rows = [mirrored(at["x"], u) for u in (1, 2, 3)]
    finish(swap(3, block, 32, others[1:4], rows))
    own.wait()


def wanted_rows(shuffle):
    return pl.pallas_call(
        wanted_kernel,
        out_shape=jax.ShapeDtypeStruct((128, 1, LANES), jnp.int32),
        in_specs=[pl.BlockSpec(memory_space=pltpu.VMEM)],
        out_specs=pl.BlockSpec(memory_space=pltpu.VMEM),
        scratch_shapes=[
            pltpu.VMEM((4, 128, 1, LANES), jnp.int32),
            pltpu.SemaphoreType.DMA((2,)),
            pltpu.SemaphoreType.DMA((4, 3)),
            pltpu.SemaphoreType.DMA((4, 3)),
        ],
        compiler_params=pltpu.CompilerParams(collective_id=1, has_side_effects=True),
    )(shuffle.reshape(4, 1, LANES))


def negatives_kernel(chunk, q_ref, bank_ref, total_ref, pull_ref):
    @pl.when(pl.program_id(0) == 0)
    def _():
        total_ref[...] = jnp.zeros_like(total_ref)
        pull_ref[...] = jnp.zeros_like(pull_ref)

    keys = bank_ref[...]
    for start in range(0, q_ref.shape[0], chunk):
        rows = slice(start, start + chunk)
        sims = lax.dot_general(
            q_ref[rows, :].astype(jnp.bfloat16), keys, (((1,), (1,)), ((), ())), preferred_element_type=jnp.float32
        )
        quarter = jnp.exp2(sims * EXP2_SCALE - 2.0)
        partial = quarter[:, 0:LANES]
        for c in range(LANES, quarter.shape[1], LANES):
            partial = partial + quarter[:, c : c + LANES]
        total_ref[rows, :] += partial
        pull_ref[rows, :] += jnp.dot(
            quarter.astype(jnp.bfloat16), keys, preferred_element_type=jnp.float32
        )


def negatives(probe_features, distractor_bank, block=4096, chunk=256):
    rows, emb = probe_features.shape
    keys = distractor_bank.shape[0]
    whole = pl.BlockSpec((rows, emb), lambda i: (0, 0))
    return pl.pallas_call(
        functools.partial(negatives_kernel, chunk),
        grid=(keys // block,),
        out_shape=(jax.ShapeDtypeStruct((rows, emb), jnp.float32),) * 2,
        in_specs=[whole, pl.BlockSpec((block, emb), lambda i: (i, 0))],
        out_specs=[whole, whole],
        cost_estimate=pl.CostEstimate(
            flops=4 * rows * keys * emb, bytes_accessed=2 * keys * emb, transcendentals=rows * keys
        ),
        compiler_params=pltpu.CompilerParams(vmem_limit_bytes=24 << 20),
    )(probe_features, distractor_bank)


def batch_stats(hidden):
    average = jnp.mean(hidden, axis=0)
    variance = jnp.mean(hidden * hidden, axis=0) - average * average
    return (average, lax.rsqrt(variance + bn_eps))


def head_tail(normed, w_out):
    active = jnp.maximum(normed, 0.0).astype(jnp.bfloat16)
    projected = jnp.einsum("gjh,he->gje", active, w_out, preferred_element_type=jnp.float32)
    return projected * lax.rsqrt(jnp.sum(projected * projected, axis=-1, keepdims=True) + norm_eps)


def key_embed(crop_rows, w_in, w_out):
    hidden = jnp.einsum("gjd,dh->gjh", crop_rows, w_in, preferred_element_type=jnp.float32)
    average = jnp.mean(hidden, axis=(0, 1))
    variance = jnp.mean(hidden * hidden, axis=(0, 1)) - average * average
    return head_tail((hidden - average) * lax.rsqrt(variance + bn_eps), w_out)


def query_forward(crop_rows, w_in, w_out):
    hidden = jnp.dot(crop_rows, w_in, preferred_element_type=jnp.float32)
    average, inv_std = batch_stats(hidden)
    normed = (hidden - average) * inv_std
    active = jnp.maximum(normed, 0.0).astype(jnp.bfloat16)
    projected = jnp.dot(active, w_out, preferred_element_type=jnp.float32)
    inv_len = lax.rsqrt(jnp.sum(projected * projected, axis=-1, keepdims=True) + norm_eps)
    stats = jnp.stack([average, inv_std])
    return (hidden, stats, inv_len, projected * inv_len)


def query_grads(crops_t, forward, lane_totals, pull, matching_targets, w_out, all_rows):
    hidden, stats, inv_len, probe_features = forward
    matching_similarity = (
        jnp.sum(probe_features * matching_targets, axis=-1, keepdims=True) / sharpness_divisor
    )
    exp_pos = jnp.exp(matching_similarity) * 0.25
    total_exp = exp_pos + jnp.sum(lane_totals, axis=-1, keepdims=True)
    scale_coef = loss_scale / all_rows
    matching_similarity_slope = scale_coef * (exp_pos / total_exp - 1.0)
    probe_feature_slope = (
        matching_similarity_slope * matching_targets + scale_coef * pull / total_exp
    ) / sharpness_divisor
    d_proj = (
        (
            probe_feature_slope
            - probe_features * jnp.sum(probe_feature_slope * probe_features, axis=-1, keepdims=True)
        )
        * inv_len
    ).astype(jnp.bfloat16)
    return summed_grads(crops_t, hidden, stats, d_proj, w_out)


def per_device(
    query_crops, key_crops, shuffle, distractor_bank, query_inner, query_outer, key_inner, key_outer
):
    group_count = lax.axis_size(("dp", "crop"))
    row_count = query_crops.shape[0]
    per_peer = row_count // group_count
    all_rows = float(row_count * group_count)
    lane = (lax.axis_index(("dp", "crop")) % 32) * per_peer
    requested = lax.dynamic_slice_in_dim(
        wanted_rows(shuffle).reshape(group_count, LANES), lane, per_peer, axis=1
    )
    flat_req = requested.reshape(-1) % row_count
    outgoing = key_crops[flat_req].reshape(group_count, per_peer, key_crops.shape[1])
    incoming = lax.all_to_all(outgoing, ("dp", "crop"), split_axis=0, concat_axis=0, tiled=True)
    forward = query_forward(query_crops, query_inner, query_outer)
    crops_t = query_crops.T
    lane_totals, pull = negatives(forward[3], distractor_bank)
    incoming, lane_totals, pull, crops_t = lax.optimization_barrier(
        (incoming, lane_totals, pull, crops_t)
    )
    embedded = key_embed(incoming, key_inner, key_outer)
    returned = lax.all_to_all(
        embedded, ("dp", "crop"), split_axis=0, concat_axis=0, tiled=True
    ).reshape(row_count, key_outer.shape[1])
    matching_targets = (
        jnp.zeros((row_count, returned.shape[1]), jnp.float32).at[flat_req].set(returned)
    )
    return query_grads(
        crops_t, forward, lane_totals, pull, matching_targets, query_outer, all_rows
    )


def solution(mesh):
    placed = (
        P(("dp", "crop"), None),
        P(("dp", "crop"), None),
        P(("dp", "crop")),
        P(),
        P(),
        P(),
        P(),
        P(),
    )
    return jax.shard_map(
        per_device,
        mesh=mesh,
        in_specs=placed,
        out_specs=(P(("dp", "crop"), None), P(("dp", "crop"), None)),
        check_vma=False,
    )
```

```python
import functools
import math
import jax
import jax.numpy as jnp
from jax import lax
from jax.experimental import pallas as pl
from jax.experimental.pallas import tpu as pltpu
from jax.sharding import PartitionSpec as P

sharpness_divisor = 0.2
loss_scale = 4096.0
bn_eps = 1e-05
norm_eps = 1e-06
EXP2_SCALE = math.log2(math.e) / sharpness_divisor


MESH = pl.DeviceIdType.MESH
CHUNK = 16
LANES = 128
TURNS = (("x", 1), ("y", 1), ("z", 1), ("x", 3), ("y", 3), ("z", 3))
BLOCK = 1024
WIDE = 4
AXES = ("x", "y", "z")


def place():
    dp, crop = lax.axis_index("dp"), lax.axis_index("crop")
    return {
        "x": dp // 8,
        "z": (dp // 2) % 4,
        "y": (dp % 2) * 2 + crop // 2,
        "core": crop % 2,
    }


def device_of(at):
    return (at["x"] * 8 + at["z"] * 2 + at["y"] // 2, (at["y"] % 2) * 2 + at["core"])


def mirrored(v, u):
    return (v, v + 1 - 2 * (v % 2), (v + 2) % 4, 3 - v)[u]


def partner(at, turn):
    if turn is None:
        return device_of({**at, "core": 1 - at["core"]})
    axis, flip = turn
    return device_of({**at, axis: mirrored(at[axis], flip)})


def plan_of(kind):
    held = {a: [0, 1, 2, 3] for a in AXES}
    hops = []
    for k in range(6):
        axis, flip = TURNS[(kind + k) % 6]
        now = held[axis]
        if len(now) == 4:
            sent = [1, 2] if flip == 1 else [3, 2]
        else:
            sent = [flip]
        kept = [u ^ flip for u in sent]
        dims = tuple(len(held[a]) for a in AXES)
        hops.append(
            (dims, AXES.index(axis), [now.index(u) for u in kept], [now.index(u) for u in sent])
        )
        held[axis] = kept
    return hops


PLANS = [plan_of(kind) for kind in range(6)]


def order_of(tiles, wide):
    steps, waiting = [], []
    first = list(range(tiles + 2))
    for g in range(tiles // wide):
        steps.append(("block", g))
        steps += [("hop", 0, t) for t in waiting]
        waiting = first[g * wide : (g + 1) * wide]
    steps.append(("outer", None))
    steps += [("hop", 0, t) for t in waiting + first[tiles:]]
    return steps + [("hop", k, t) for k in range(1, 7) for t in first]


def grads_kernel(
    tiles,
    xt_any,
    hid_any,
    stats_ref,
    dz_ref,
    w_ref,
    out_ref,
    xt_ref,
    hid_ref,
    go_ref,
    load_sem,
    xp,
    slope,
    *rest,
):
    acc, send, recv = rest[0:7], rest[7:14], rest[14:21]
    send_sem, recv_sem = rest[21], rest[22]
    slots = tiles + 2
    at = place()
    barrier = pltpu.get_barrier_semaphore()
    for turn in (None,) + TURNS:
        pl.semaphore_signal(barrier, inc=1, device_id=partner(at, turn), device_id_type=MESH)

    def columns(g):
        return slice(WIDE * g * LANES, (g + 1) * WIDE * LANES)

    blocks = tiles // WIDE
    loads = [
        pltpu.make_async_copy(hid_any.at[:, columns(g)], hid_ref.at[g], load_sem.at[g])
        for g in range(blocks)
    ]
    loads.append(pltpu.make_async_copy(xt_any, xt_ref, load_sem.at[blocks]))
    for i in (blocks, *range(blocks)):
        loads[i].start()
    loads[blocks].wait()

    def copy(k, t, kind):
        turn = None if k == 0 else TURNS[(kind + k - 1) % 6]
        return pltpu.make_async_remote_copy(
            src_ref=send[k].at[t],
            dst_ref=recv[k].at[t],
            send_sem=send_sem.at[k, t],
            recv_sem=recv_sem.at[k, t],
            device_id=partner(at, turn),
            device_id_type=MESH,
        )

    def combine(k, t, kind):
        copy(k, t, kind).wait_recv()
        total = acc[k][t] + recv[k][t].astype(jnp.float32)
        if k == 6:
            return total[0]
        dims, axis, kept, sent = PLANS[kind][k]
        total = total.reshape(dims + (CHUNK, LANES))
        out_dims = tuple(n // 2 if i == axis else n for i, n in enumerate(dims))

        def pick(positions):
            parts = [lax.slice_in_dim(total, p, p + 1, axis=axis) for p in positions]
            joined = parts[0] if len(parts) == 1 else jnp.concatenate(parts, axis=axis)
            return joined.reshape((-1, CHUNK, LANES))

        send[k + 1][t] = pick(sent).astype(jnp.bfloat16)
        acc[k + 1][t] = pick(kept)
        copy(k + 1, t, kind).start()

    rows = {}
    index = 0
    for far in (1, 0):
        core = at["core"] if far == 0 else 1 - at["core"]
        for ux in range(4):
            for uy in range(4):
                for uz in range(4):
                    wx, wy, wz = (mirrored(at[a], u) for a, u in zip(AXES, (ux, uy, uz)))
                    row = pl.multiple_of((((wx * 4 + wz) * 4 + wy) * 2 + core) * CHUNK, CHUNK)
                    rows[index] = row
                    xp[index * CHUNK : (index + 1) * CHUNK, :] = xt_ref[pl.ds(row, CHUNK), :]
                    index += 1

    def outer():
        for i in range(64):
            send[0][tiles, i] = go_ref[pl.ds(rows[i], CHUNK), :].astype(jnp.bfloat16)
            acc[0][tiles, i] = go_ref[pl.ds(rows[64 + i], CHUNK), :]
        send[0][tiles + 1] = jnp.zeros((64, CHUNK, LANES), jnp.bfloat16)
        acc[0][tiles + 1] = jnp.zeros((64, CHUNK, LANES), jnp.float32)
        for t in (tiles, tiles + 1):
            copy(0, t, t % 6).start()

    def inner(g):
        cols = columns(g)
        loads[g].wait()
        inv_std = stats_ref[1:2, cols]
        normed = (hid_ref[g] - stats_ref[0:1, cols]) * inv_std
        d_act = lax.dot_general(
            dz_ref[...], w_ref[cols, :], (((1,), (1,)), ((), ())), preferred_element_type=jnp.float32
        )
        d_norm = jnp.where(normed > 0.0, d_act, 0.0)
        d_mean = jnp.mean(d_norm, axis=0, keepdims=True)
        d_pull = jnp.mean(d_norm * normed, axis=0, keepdims=True)
        slope[g % 2] = (inv_std * (d_norm - d_mean - normed * d_pull)).astype(jnp.bfloat16)
        right = slope[g % 2]

        def block(far, b):
            size = BLOCK // CHUNK
            first = pl.multiple_of(far * 1024 + b * BLOCK, BLOCK)
            left = xp[pl.ds(first, BLOCK), :]
            part = jnp.dot(left, right, preferred_element_type=jnp.float32)
            for h in range(WIDE):
                half = part[:, h * LANES : (h + 1) * LANES].reshape(size, CHUNK, LANES)
                where = pl.ds(b * size, size)
                if far == 0:
                    send[0][WIDE * g + h, where] = half.astype(jnp.bfloat16)
                else:
                    acc[0][WIDE * g + h, where] = half

        for far in (0, 1):
            if BLOCK == 1024:
                block(far, 0)
            else:

                @pl.loop(0, 1024 // BLOCK)
                def _(b, far=far):
                    block(far, b)

            if far == 0:
                if g == 0:
                    pl.semaphore_wait(barrier, 1 + len(TURNS))
                for t in range(WIDE * g, WIDE * (g + 1)):
                    copy(0, t, t % 6).start()

        active = jnp.maximum(normed, 0.0).astype(jnp.bfloat16)
        turned = lax.dot_general(
            dz_ref[...], active, (((0,), (0,)), ((), ())), preferred_element_type=jnp.float32
        )
        go_ref[cols, :] = jnp.transpose(turned)

    for step in order_of(tiles, WIDE):
        if step[0] == "outer":
            outer()
        elif step[0] == "block":
            inner(step[1])
        else:
            _, k, t = step
            done = combine(k, t, t % 6)
            if k == 6 and t <= tiles:
                out_ref[:, t * LANES : (t + 1) * LANES] = done

    for k in range(7):

        @pl.loop(0, slots // 6)
        def _(r, k=k):
            for kind in range(6):
                copy(k, r * 6 + kind, kind).wait_send()


def summed_grads(crops_t, hidden, stats, d_proj, w_out):
    depth, batch = crops_t.shape
    width = hidden.shape[1]
    tiles = width // LANES
    slots = tiles + 2

    def slabs(dtype):
        return [pltpu.VMEM((slots, 64 >> k, CHUNK, LANES), dtype) for k in range(7)]

    summed = pl.pallas_call(
        functools.partial(grads_kernel, tiles),
        out_shape=jax.ShapeDtypeStruct((CHUNK, width + LANES), jnp.float32),
        in_specs=[pl.BlockSpec(memory_space=pl.ANY)] * 2
        + [pl.BlockSpec(memory_space=pltpu.VMEM)] * 3,
        out_specs=pl.BlockSpec(memory_space=pltpu.VMEM),
        scratch_shapes=[
            pltpu.VMEM((depth, batch), jnp.bfloat16),
            pltpu.VMEM((tiles // WIDE, batch, WIDE * LANES), jnp.float32),
            pltpu.VMEM((width, LANES), jnp.float32),
            pltpu.SemaphoreType.DMA((tiles // WIDE + 1,)),
            pltpu.VMEM((depth, batch), jnp.bfloat16),
            pltpu.VMEM((2, batch, WIDE * LANES), jnp.bfloat16),
        ]
        + slabs(jnp.float32)
        + slabs(jnp.bfloat16)
        + slabs(jnp.bfloat16)
        + [pltpu.SemaphoreType.DMA((7, slots)), pltpu.SemaphoreType.DMA((7, slots))],
        compiler_params=pltpu.CompilerParams(
            collective_id=0, has_side_effects=True, vmem_limit_bytes=56 << 20
        ),
    )(crops_t, hidden, stats, d_proj, w_out)
    return (summed[:, :width], summed[:, width:])


def wanted_kernel(order_ref, out_ref, table, keep_sem, send_sem, recv_sem):
    at = place()
    barrier = pltpu.get_barrier_semaphore()
    others = [device_of({**at, "core": 1 - at["core"]})]
    for axis in AXES:
        others += [device_of({**at, axis: mirrored(at[axis], u)}) for u in (1, 2, 3)]
    for other in others:
        pl.semaphore_signal(barrier, inc=1, device_id=other, device_id_type=MESH)
    pl.semaphore_wait(barrier, len(others))

    mine = at["x"] * 32 + at["z"] * 8 + at["y"] * 2 + at["core"]
    keep = pltpu.make_async_copy(order_ref, table.at[:, mine], keep_sem.at[0])
    keep.start()

    def swap(phase, first, count, targets, sources=None):
        copies = []
        for i, target in enumerate(targets):
            if sources is None:
                part = (slice(None), pl.ds(first, count))
                source, landing = table.at[part], table.at[part]
            else:
                source = table.at[sources[i], pl.ds(first, count)]
                landing = out_ref.at[pl.ds(first, count)]
            copies.append(
                pltpu.make_async_remote_copy(
                    src_ref=source,
                    dst_ref=landing,
                    send_sem=send_sem.at[phase, i],
                    recv_sem=recv_sem.at[phase, i],
                    device_id=target,
                    device_id_type=MESH,
                )
            )
        for copy in copies:
            copy.start()
        return copies

    def finish(copies):
        for copy in copies:
            copy.wait()

    first = pltpu.make_async_remote_copy(
        src_ref=order_ref,
        dst_ref=table.at[:, mine],
        send_sem=send_sem.at[0, 0],
        recv_sem=recv_sem.at[0, 0],
        device_id=others[0],
        device_id_type=MESH,
    )
    first.start()
    keep.wait()
    first.wait()
    finish(swap(1, mine - mine % 2, 2, others[4:7]))
    finish(swap(2, mine - mine % 8, 8, others[7:10]))
    block = at["x"] * 32
    own = pltpu.make_async_copy(
        table.at[at["x"], pl.ds(block, 32)], out_ref.at[pl.ds(block, 32)], keep_sem.at[1]
    )
    own.start()
    rows = [mirrored(at["x"], u) for u in (1, 2, 3)]
    finish(swap(3, block, 32, others[1:4], rows))
    own.wait()


def wanted_rows(shuffle):
    return pl.pallas_call(
        wanted_kernel,
        out_shape=jax.ShapeDtypeStruct((128, 1, LANES), jnp.int32),
        in_specs=[pl.BlockSpec(memory_space=pltpu.VMEM)],
        out_specs=pl.BlockSpec(memory_space=pltpu.VMEM),
        scratch_shapes=[
            pltpu.VMEM((4, 128, 1, LANES), jnp.int32),
            pltpu.SemaphoreType.DMA((2,)),
            pltpu.SemaphoreType.DMA((4, 3)),
            pltpu.SemaphoreType.DMA((4, 3)),
        ],
        compiler_params=pltpu.CompilerParams(collective_id=1, has_side_effects=True),
    )(shuffle.reshape(4, 1, LANES))


def negatives_kernel(chunk, q_ref, bank_ref, total_ref, pull_ref):
    @pl.when(pl.program_id(0) == 0)
    def _():
        total_ref[...] = jnp.zeros_like(total_ref)
        pull_ref[...] = jnp.zeros_like(pull_ref)

    keys = bank_ref[...]
    for start in range(0, q_ref.shape[0], chunk):
        rows = slice(start, start + chunk)
        sims = lax.dot_general(
            q_ref[rows, :].astype(jnp.bfloat16), keys, (((1,), (1,)), ((), ())), preferred_element_type=jnp.float32
        )
        quarter = jnp.exp2(sims * EXP2_SCALE - 2.0)
        partial = quarter[:, 0:LANES]
        for c in range(LANES, quarter.shape[1], LANES):
            partial = partial + quarter[:, c : c + LANES]
        total_ref[rows, :] += partial
        pull_ref[rows, :] += jnp.dot(
            quarter.astype(jnp.bfloat16), keys, preferred_element_type=jnp.float32
        )


def negatives(probe_features, distractor_bank, block=4096, chunk=256):
    rows, emb = probe_features.shape
    keys = distractor_bank.shape[0]
    whole = pl.BlockSpec((rows, emb), lambda i: (0, 0))
    return pl.pallas_call(
        functools.partial(negatives_kernel, chunk),
        grid=(keys // block,),
        out_shape=(jax.ShapeDtypeStruct((rows, emb), jnp.float32),) * 2,
        in_specs=[whole, pl.BlockSpec((block, emb), lambda i: (i, 0))],
        out_specs=[whole, whole],
        cost_estimate=pl.CostEstimate(
            flops=4 * rows * keys * emb, bytes_accessed=2 * keys * emb, transcendentals=rows * keys
        ),
        compiler_params=pltpu.CompilerParams(vmem_limit_bytes=24 << 20),
    )(probe_features, distractor_bank)


def batch_stats(hidden):
    average = jnp.mean(hidden, axis=0)
    variance = jnp.mean(hidden * hidden, axis=0) - average * average
    return (average, lax.rsqrt(variance + bn_eps))


def head_tail(normed, w_out):
    active = jnp.maximum(normed, 0.0).astype(jnp.bfloat16)
    projected = jnp.einsum("gjh,he->gje", active, w_out, preferred_element_type=jnp.float32)
    return projected * lax.rsqrt(jnp.sum(projected * projected, axis=-1, keepdims=True) + norm_eps)


def key_embed(crop_rows, w_in, w_out):
    hidden = jnp.einsum("gjd,dh->gjh", crop_rows, w_in, preferred_element_type=jnp.float32)
    average = jnp.mean(hidden, axis=(0, 1))
    variance = jnp.mean(hidden * hidden, axis=(0, 1)) - average * average
    return head_tail((hidden - average) * lax.rsqrt(variance + bn_eps), w_out)


def query_forward(crop_rows, w_in, w_out):
    hidden = jnp.dot(crop_rows, w_in, preferred_element_type=jnp.float32)
    average, inv_std = batch_stats(hidden)
    normed = (hidden - average) * inv_std
    active = jnp.maximum(normed, 0.0).astype(jnp.bfloat16)
    projected = jnp.dot(active, w_out, preferred_element_type=jnp.float32)
    inv_len = lax.rsqrt(jnp.sum(projected * projected, axis=-1, keepdims=True) + norm_eps)
    stats = jnp.stack([average, inv_std])
    return (hidden, stats, inv_len, projected * inv_len)


def query_grads(crops_t, forward, lane_totals, pull, matching_targets, w_out, all_rows):
    hidden, stats, inv_len, probe_features = forward
    matching_similarity = (
        jnp.sum(probe_features * matching_targets, axis=-1, keepdims=True) / sharpness_divisor
    )
    exp_pos = jnp.exp(matching_similarity) * 0.25
    total_exp = exp_pos + jnp.sum(lane_totals, axis=-1, keepdims=True)
    scale_coef = loss_scale / all_rows
    matching_similarity_slope = scale_coef * (exp_pos / total_exp - 1.0)
    probe_feature_slope = (
        matching_similarity_slope * matching_targets + scale_coef * pull / total_exp
    ) / sharpness_divisor
    d_proj = (
        (
            probe_feature_slope
            - probe_features * jnp.sum(probe_feature_slope * probe_features, axis=-1, keepdims=True)
        )
        * inv_len
    ).astype(jnp.bfloat16)
    return summed_grads(crops_t, hidden, stats, d_proj, w_out)


def per_device(
    query_crops, key_crops, shuffle, distractor_bank, query_inner, query_outer, key_inner, key_outer
):
    group_count = lax.axis_size(("dp", "crop"))
    row_count = query_crops.shape[0]
    per_peer = row_count // group_count
    all_rows = float(row_count * group_count)
    lane = (lax.axis_index(("dp", "crop")) % 32) * per_peer
    requested = lax.dynamic_slice_in_dim(
        wanted_rows(shuffle).reshape(group_count, LANES), lane, per_peer, axis=1
    )
    flat_req = requested.reshape(-1) % row_count
    outgoing = key_crops[flat_req].reshape(group_count, per_peer, key_crops.shape[1])
    incoming = lax.all_to_all(outgoing, ("dp", "crop"), split_axis=0, concat_axis=0, tiled=True)
    forward = query_forward(query_crops, query_inner, query_outer)
    crops_t = query_crops.T
    lane_totals, pull = negatives(forward[3], distractor_bank)
    incoming, lane_totals, pull, crops_t = lax.optimization_barrier(
        (incoming, lane_totals, pull, crops_t)
    )
    embedded = key_embed(incoming, key_inner, key_outer)
    returned = lax.all_to_all(
        embedded, ("dp", "crop"), split_axis=0, concat_axis=0, tiled=True
    ).reshape(row_count, key_outer.shape[1])
    matching_targets = (
        jnp.zeros((row_count, returned.shape[1]), jnp.float32).at[flat_req].set(returned)
    )
    return query_grads(
        crops_t, forward, lane_totals, pull, matching_targets, query_outer, all_rows
    )


def solution(mesh):
    placed = (
        P(("dp", "crop"), None),
        P(("dp", "crop"), None),
        P(("dp", "crop")),
        P(),
        P(),
        P(),
        P(),
        P(),
    )
    return jax.shard_map(
        per_device,
        mesh=mesh,
        in_specs=placed,
        out_specs=(P(("dp", "crop"), None), P(("dp", "crop"), None)),
        check_vma=False,
    )
```
